128 devices in a mesh: wide: 8 (over x, y_hi), narrow: 16 (over y_lo, z, core).
Axes of the slice: x: 4, y: 4 (y_hi: 2, y_lo: 2; y = y_hi * 2 + y_lo), z: 4, core: 2. Of those that a mesh axis runs over, the one named last changes fastest.
Arguments:
- volume_field: float32 [2, 8, 128, 256, 512], P(None, None, 'wide', 'narrow'), may hold values from -6 to 6
- coefficients: bfloat16 [3, 128, 256, 512], P(None, 'wide', 'narrow'), may hold values from 0.25 to 1
- density: float32 [2, 8, 65536], P(None, None, 'narrow'), may hold values from -6 to 6
- boundary_matrix: bfloat16 [2, 4, 512, 65536], P(None, None, 'wide', 'narrow'), may hold values from -0.03125 to 0.03125
- upsample: int32 [128], P('narrow'), may hold values from 1 to 4, as said below
- trace_cell: int32 [8, 16, 256], P('wide', 'narrow'), may hold values from 0 to 255
- trace_row: int32 [8, 16, 256], P('wide', 'narrow'), may hold values from 0 to 511, as said below
- slot_counts: int32 [8, 16], P('wide', 'narrow'), may hold values from 192 to 256, as said below
Outputs:
- volume_out: float32 [2, 8, 128, 256, 512], P(None, None, 'wide', 'narrow')
- boundary_out: float32 [2, 8, 512], P(None, None, ('wide', 'narrow'))
The draws below stay inside these ranges and needn't reach their ends.
Inputs may be any that keep to these rules, and one draw needn't show every extreme that they name: `trace_row`: live slots of one brick name rows of one owner (rows k * 4 to (k + 1) * 4 - 1) at most 4 times; in every draw one owner is named 4 times by the live slots of every brick. `slot_counts`: some brick has all 256 slots live. `upsample`: some panel group has factor 4 and some has factor 1.
All inputs are finite; a program needn't handle non-finite values.
Results may differ from the reference program's by a relative error of at most 0.0019.
Values sent between devices are 32-bit elements; how exact they have to be, the bound alone decides.
No kernel may reach another device: no remote copies, remote signals or barrier semaphores. Data moves between devices by JAX's collectives and lax.ppermute only.
A program may use at most 192 MiB of HBM per device.

```python
import jax
import jax.numpy as jnp
from jax import lax

W = 8
CX = 16
CY = 16
NZ = 512
NB = 65536
COLS_BLK = 512
UMAX = 4
TSLOTS = 256
CAP = 4
NX = 128
NY = 256
ROWS = 512
RPD = 4
BLOCKS = 128
N_WIDE = 8
N_NARROW = 16


def slot_plan(key):
    device_count = N_WIDE * N_NARROW
    key_hot, key_bricks, key_full = jax.random.split(key, 3)
    hottest = jax.random.randint(key_hot, (), 0, device_count)
    full_brick = jax.random.randint(key_full, (), 0, device_count)

    def one_brick(brick_key, brick):
        key_order, key_count, key_shuffle, key_local = jax.random.split(brick_key, 4)
        order = jax.random.permutation(key_order, CAP * (device_count - 1))[:TSLOTS - CAP]
        owner_rest = (hottest + 1 + order % (device_count - 1)) % device_count
        owners = jnp.concatenate([jnp.full((CAP,), hottest, jnp.int32), owner_rest.astype(jnp.int32)])
        live_count = jax.random.randint(key_count, (), 3 * TSLOTS // 4, TSLOTS + 1)
        live_count = jnp.where(brick == full_brick, TSLOTS, live_count)
        position = jnp.arange(TSLOTS, dtype=jnp.int32)
        scores = jax.random.randint(key_shuffle, (TSLOTS,), 0, TSLOTS) * TSLOTS + position
        scores = jnp.where(position < live_count, scores, TSLOTS * TSLOTS + position)
        shuffled = jnp.argsort(scores, stable=True)
        owners = owners[shuffled]
        local_row = jax.random.randint(key_local, (TSLOTS,), 0, RPD)
        return ((owners * RPD + local_row).astype(jnp.int32), live_count.astype(jnp.int32))
    brick_keys = jax.random.split(key_bricks, device_count)
    slot_rows, live_counts = jax.vmap(one_brick)(brick_keys, jnp.arange(device_count, dtype=jnp.int32))
    return (slot_rows.reshape(N_WIDE, N_NARROW, TSLOTS), live_counts.reshape(N_WIDE, N_NARROW))


def draw_trace_row(key, part):
    return slot_plan(jax.random.fold_in(key, 7))[0]


def draw_slot_counts(key, part):
    return slot_plan(jax.random.fold_in(key, 7))[1]


def draw_upsample(key, part):
    key_base, key_start = jax.random.split(key)
    base = jax.random.randint(key_base, (BLOCKS,), 1, 3)
    start = jax.random.randint(key_start, (), 0, BLOCKS)
    run_length = max(BLOCKS // 8, 1)
    position = (jnp.arange(BLOCKS, dtype=jnp.int32) - start) % BLOCKS
    values = jnp.where(position < run_length, UMAX, base)
    values = jnp.where(position == run_length, 1, values)
    return values.astype(jnp.int32)


def plant(drawn, stream_key, low, largest):
    shape = drawn.shape
    index_at = [jax.random.randint(jax.random.fold_in(stream_key, axis), (), 0, shape[axis]) for axis in range(len(shape))]
    drawn = drawn.at[tuple(index_at)].set(low)
    longest = shape.index(max(shape))
    index_at[longest] = (index_at[longest] + 1) % shape[longest]
    return drawn.at[tuple(index_at)].set(largest)


def strengthened(entries, own_key, source, target, blocks, factor):
    owner, partner = [(jnp.arange(entries.shape[axis_at]) // (entries.shape[axis_at] // blocks)).reshape([-1 if axis == axis_at else 1 for axis in range(entries.ndim)]) for axis_at in (source, target)]
    chosen = jax.random.permutation(own_key, blocks)[partner]
    strong = (owner == chosen) | (owner == (partner + blocks // 2) % blocks)
    return jnp.where(strong, factor * entries, entries)


def levels(rng, extent, pieces, low, largest):
    def one(axis_at, parts):
        steps = jax.random.uniform(jax.random.fold_in(jax.random.fold_in(rng, 6), axis_at), (parts,), jnp.float32, low / len(pieces), largest / len(pieces))
        return jnp.repeat(jnp.exp(steps), extent[axis_at] // parts).reshape((-1,) + (1,) * (len(extent) - axis_at - 1))

    factor_of = one(*pieces[0])
    for cut in pieces[1:]:
        factor_of = factor_of * one(*cut)
    return factor_of


def centred(stream_key, extent, scale, most, pieces=(), held_as=jnp.bfloat16):
    values = jax.random.normal(stream_key, extent, jnp.float32) * scale
    if len(pieces) > 0:
        values = levels(stream_key, extent, pieces, -0.22, 0.18) * values
    return jnp.clip(values, min=-most, max=most).astype(held_as)


def heavy_noise(rng, shape, spread, most, cuts, heavy, kind=jnp.bfloat16):
    drawn = spread * jax.random.normal(rng, shape, jnp.float32)
    if cuts:
        drawn = drawn * levels(rng, shape, cuts, -0.22, 0.18)
    return jnp.clip(strengthened(drawn, jax.random.fold_in(rng, 3), *heavy), -most, most).astype(kind)


def setup_inputs(seed: int = 0) -> dict:
    arg_keys = jax.random.split(jax.random.key(seed), 9)
    volume_field = centred(arg_keys[0], (2, W, NX, NY, NZ), 1.0, 6.0, ((2, 8), (3, 16)), jnp.float32)
    coefficients = jnp.clip(0.25 + 0.75 * jax.random.uniform(arg_keys[1], (3, NX, NY, NZ), jnp.float32) ** levels(arg_keys[1], (3, NX, NY, NZ), ((1, 8), (2, 16)), -0.2, 0.2), 0.25, 1.0).astype(jnp.bfloat16)
    density = centred(arg_keys[2], (2, W, NB), 1.0, 6.0, ((2, 16),), jnp.float32)
    boundary_matrix = heavy_noise(arg_keys[3], (2, UMAX, ROWS, NB), NB ** -0.5, 0.03125, ((2, 8), (3, 16)), (3, 2, 16, 2.0))
    upsample = draw_upsample(jax.random.fold_in(arg_keys[8], 71), 0)
    trace_cell = plant(jax.random.randint(arg_keys[5], (N_WIDE, N_NARROW, TSLOTS), 0, CX * CY), jax.random.fold_in(arg_keys[5], 1), 0, (CX * CY) - 1).astype(jnp.int32)
    trace_row = draw_trace_row(jax.random.fold_in(arg_keys[8], 71), 0)
    slot_counts = draw_slot_counts(jax.random.fold_in(arg_keys[8], 71), 0)
    return {"volume_field": volume_field, "coefficients": coefficients, "density": density, "boundary_matrix": boundary_matrix, "upsample": upsample, "trace_cell": trace_cell, "trace_row": trace_row, "slot_counts": slot_counts}


def channel_stiffness(plane):
    padded = jnp.pad(plane, 1)
    size_x, size_y, size_z = plane.shape
    edge_sum = jnp.zeros(plane.shape, jnp.float32)
    corner_sum = jnp.zeros(plane.shape, jnp.float32)
    for across in (-1, 0, 1):
        for along in (-1, 0, 1):
            for upward in (-1, 0, 1):
                moved = abs(across) + abs(along) + abs(upward)
                if moved < 2:
                    continue
                shifted = padded[1 + across:1 + across + size_x, 1 + along:1 + along + size_y, 1 + upward:1 + upward + size_z]
                if moved == 2:
                    edge_sum = edge_sum + shifted
                else:
                    corner_sum = corner_sum + shifted
    return (8.0 / 3.0) * plane - edge_sum / 6.0 - corner_sum / 12.0


def reference(volume_field, coefficients, density, boundary_matrix, upsample, trace_cell, trace_row, slot_counts):
    channels = volume_field.reshape(2 * W, NX, NY, NZ)
    stiffness = lax.map(channel_stiffness, channels).reshape(volume_field.shape)
    scales = coefficients.astype(jnp.float32)
    turned = jnp.stack([volume_field[1], -volume_field[0]])
    operated = scales[0] * stiffness - scales[1] * volume_field + scales[2] * turned

    blocks_density = density.reshape(2 * W, BLOCKS, COLS_BLK)
    following = jnp.concatenate([blocks_density[:, :, 1:], blocks_density[:, :, -1:]], axis=2)
    factor = upsample.astype(jnp.float32)[None, :, None]
    products = jnp.zeros((2 * ROWS, 2 * W), jnp.float32)
    for level_index in range(UMAX):
        blend = level_index / factor
        fine = jnp.where(level_index < upsample[None, :, None], ((1.0 - blend) * blocks_density + blend * following) / factor, 0.0)
        fine = fine.reshape(2 * W, NB).astype(jnp.bfloat16)
        matrix = boundary_matrix[:, level_index].reshape(2 * ROWS, NB)
        products = products + lax.dot_general(matrix, fine, (((1,), (1,)), ((), ())), preferred_element_type=jnp.float32)
    real_rows = products[:ROWS, :W] - products[ROWS:, W:]
    imag_rows = products[:ROWS, W:] + products[ROWS:, :W]
    bem_rows = jnp.concatenate([real_rows, imag_rows], axis=1)

    slot_index = jnp.arange(TSLOTS, dtype=jnp.int32)
    live_mask = (slot_index[None, None, :] < slot_counts[:, :, None]).reshape(-1)
    cell_x = (jnp.arange(N_WIDE, dtype=jnp.int32)[:, None, None] * CX + trace_cell // CY).reshape(-1)
    cell_y = (jnp.arange(N_NARROW, dtype=jnp.int32)[None, :, None] * CY + trace_cell % CY).reshape(-1)
    slot_rows = trace_row.reshape(-1).astype(jnp.int32)
    top_plane = volume_field[:, :, :, :, NZ - 1].reshape(2 * W, NX * NY)
    cell_ids = (cell_x * NY + cell_y).astype(jnp.int32)
    slot_values = jnp.where(live_mask[:, None], top_plane[:, cell_ids].T, 0.0)
    trace_sum = jax.ops.segment_sum(slot_values, slot_rows, num_segments=ROWS)
    boundary_out = (bem_rows - 0.25 * trace_sum).T.reshape(2, W, ROWS)

    sent_back = jnp.where(live_mask[:, None], bem_rows[slot_rows], 0.0)
    cell_add = jax.ops.segment_sum(sent_back, cell_ids, num_segments=NX * NY)
    cell_add = cell_add.T.reshape(2, W, NX, NY)
    volume_out = operated.at[:, :, :, :, NZ - 1].add(cell_add)
    return volume_out, boundary_out
```

```python
from functools import partial

import jax
import jax.numpy as jnp
from jax import lax
from jax.experimental import pallas as pl
from jax.experimental.pallas import tpu as pltpu
from jax.sharding import PartitionSpec as P

UMAX = 4
F32 = jnp.float32
BF16 = jnp.bfloat16
NT = (((1,), (1,)), ((), ()))
NN = (((1,), (0,)), ((), ()))


def split3(value):
    high = value.astype(BF16)
    rest = value - high.astype(F32)
    middle = rest.astype(BF16)
    low = (rest - middle.astype(F32)).astype(BF16)
    return high, middle, low


def front_kernel(
    upsample, counts, density, matrix, top, cells, rows, bem_out, trace_out, count_out, acc
):
    block = pl.program_id(0)
    wide = lax.axis_index("wide")

    @pl.when(block == 0)
    def _():
        acc[...] = jnp.zeros_like(acc)
        slots = cells.shape[1]
        cell_count, row_count = count_out.shape
        live = lax.broadcasted_iota(jnp.int32, (1, slots), 1) < counts[0, 0]
        cell_of = jnp.where(live, cells[...], -1)
        cell_hit = lax.broadcasted_iota(jnp.int32, (cell_count, slots), 0) == cell_of
        row_of = rows[...] ^ (wide * (row_count // 8))
        row_hit = lax.broadcasted_iota(jnp.int32, (row_count, slots), 0) == row_of
        one = jnp.ones((), F32)
        zero = jnp.zeros((), F32)
        cell_hit = jnp.where(cell_hit, one, zero).astype(BF16)
        row_hit = jnp.where(row_hit, one, zero).astype(BF16)
        counted = lax.dot_general(cell_hit, row_hit, NT, preferred_element_type=F32)
        counted = counted.astype(BF16)
        count_out[...] = counted
        total = jnp.zeros((top.shape[0], row_count), F32)
        for piece in reversed(split3(top[...])):
            total = total + lax.dot_general(piece, counted, NN, preferred_element_type=F32)
        for part in range(trace_out.shape[0]):
            trace_out[part] = total[:, part * 128 : (part + 1) * 128]

    factor_whole = upsample[block]
    own = density[...]
    width = own.shape[1]
    lane = lax.broadcasted_iota(jnp.int32, own.shape, 1)
    following = jnp.where(lane == width - 1, own, pltpu.roll(own, width - 1, 1))
    factor = jnp.full(own.shape, factor_whole, jnp.int32).astype(F32)
    total = acc[...]
    for level in range(UMAX):
        blend = level / factor
        fine = ((1.0 - blend) * own + blend * following) / factor
        fine = jnp.where(level < factor_whole, fine, 0.0).astype(BF16)
        both = matrix[:, level].reshape(2 * matrix.shape[2], width)
        total = total + lax.dot_general(fine, both, NT, preferred_element_type=F32)
    acc[...] = total

    @pl.when(block == pl.num_programs(0) - 1)
    def _():
        waves = total.shape[0] // 2
        group = total.shape[1] // 2
        turned = pltpu.roll(total, group, 1)
        bem_out[:waves] = total[:waves] - turned[waves:]
        bem_out[waves:] = total[waves:] + turned[:waves]


def front(upsample, counts, density, matrix, top, cells, rows):
    blocks = upsample.shape[0]
    channels, columns = density.shape
    width = columns // blocks
    group = matrix.shape[2]
    return pl.pallas_call(
        front_kernel,
        grid=(blocks,),
        in_specs=[
            pl.BlockSpec(memory_space=pltpu.SMEM),
            pl.BlockSpec(memory_space=pltpu.SMEM),
            pl.BlockSpec((channels, width), lambda b: (0, b)),
            pl.BlockSpec((2, UMAX, group, width), lambda b: (0, 0, 0, b)),
            pl.BlockSpec((channels, 256), lambda b: (0, 0)),
            pl.BlockSpec((1, 256), lambda b: (0, 0)),
            pl.BlockSpec((1, 256), lambda b: (0, 0)),
        ],
        out_specs=[
            pl.BlockSpec((channels, 128), lambda b: (0, 0)),
            pl.BlockSpec((4, channels, 128), lambda b: (0, 0, 0)),
            pl.BlockSpec((256, 512), lambda b: (0, 0)),
        ],
        out_shape=[
            jax.ShapeDtypeStruct((channels, 128), F32),
            jax.ShapeDtypeStruct((4, channels, 128), F32),
            jax.ShapeDtypeStruct((256, 512), BF16),
        ],
        scratch_shapes=[pltpu.VMEM((channels, 128), F32)],
        name="front",
    )(upsample, counts, density, matrix, top, cells, rows)


def y_sum(value, before, after):
    size = value.shape[0]
    at = lax.broadcasted_iota(jnp.int32, value.shape, 0)
    down = jnp.where(at == 0, before, pltpu.roll(value, 1, 0))
    up = jnp.where(at == size - 1, after, pltpu.roll(value, size - 1, 0))
    return down + up


def z_sum(value):
    size = value.shape[1]
    at = lax.broadcasted_iota(jnp.int32, value.shape, 1)
    down = jnp.where(at == 0, 0.0, pltpu.roll(value, 1, 1))
    up = jnp.where(at == size - 1, 0.0, pltpu.roll(value, size - 1, 1))
    return down + up


def interior_kernel(*refs):
    volume, coefficients, before, after = refs[:4]
    out = refs[-1]
    size_x = volume.shape[2]

    def plane(x, has_before, has_after):
        scale = coefficients[0, x].astype(F32)
        wave = coefficients[1, x].astype(F32)
        absorb = coefficients[2, x].astype(F32)
        twelfth = scale * (1.0 / 12.0)
        diagonal = scale * (8.0 / 3.0) - wave

        def across(load):
            if has_before and has_after:
                return load(x - 1) + load(x + 1)
            return load(x - 1) if has_before else load(x + 1)

        results = []
        for part in range(2):
            centre = volume[part, 0, x]
            sides = across(lambda i: volume[part, 0, i])

            def row(ref, i):
                return ref[part, 0, pl.ds(i, 1), :]

            low_sides = across(lambda i: row(before, i))
            high_sides = across(lambda i: row(after, i))
            low_mixed = low_sides + 2.0 * row(before, x)
            high_mixed = high_sides + 2.0 * row(after, x)
            twice = y_sum(sides, low_sides, high_sides)
            mixed = y_sum(sides + 2.0 * centre, low_mixed, high_mixed)
            near = z_sum(mixed + 2.0 * sides) + 2.0 * twice
            results.append((centre, diagonal * centre - twelfth * near))
        (real, real_out), (imag, imag_out) = results
        out[0, 0, x] = real_out + absorb * imag
        out[1, 0, x] = imag_out - absorb * real

    plane(0, False, True)

    def step(x, carry):
        plane(x, True, True)
        return carry

    lax.fori_loop(1, size_x - 1, step, 0)
    plane(size_x - 1, True, False)


def interior(volume, coefficients, before, after, first, count, previous=None):
    parts, waves, size_x, size_y, size_z = volume.shape
    whole = pl.BlockSpec((parts, 1, size_x, size_y, size_z), lambda i: (0, first + i, 0, 0, 0))
    face = pl.BlockSpec((parts, 1, size_x, size_z), lambda i: (0, first + i, 0, 0))
    fixed = pl.BlockSpec(coefficients.shape, lambda i: (0, 0, 0, 0))
    specs = [whole, fixed, face, face]
    operands = [volume, coefficients, before, after]
    aliases = {}
    if previous is not None:
        specs.append(pl.BlockSpec(memory_space=pl.ANY))
        operands.append(previous)
        aliases = {4: 0}
    return pl.pallas_call(
        interior_kernel,
        grid=(count,),
        in_specs=specs,
        out_specs=whole,
        out_shape=jax.ShapeDtypeStruct(volume.shape, F32),
        input_output_aliases=aliases,
        name="interior",
    )(*operands)


def final_kernel(
    coefficients,
    same_plane,
    same_corner,
    cross_plane,
    small,
    counted,
    started,
    out,
    boundary,
    planes,
    tops,
    sems,
):
    wide = lax.axis_index("wide")
    narrow = lax.axis_index("narrow")
    size_x = out.shape[2]
    even = wide % 2 == 0
    last = size_x - 1
    same_x = jnp.where(even, last, 0)
    cross_x = jnp.where(even, 0, last)
    places = (same_x, cross_x)
    channels = boundary.shape[0]
    waves = channels // 2
    low = out.shape[4] - 128

    def plane_copy(side, inward):
        there = out.at[:, :, places[side]]
        here = planes.at[side]
        pair = (there, here) if inward else (here, there)
        return pltpu.make_async_copy(*pair, sems.at[side])

    def top_copy(inward):
        there = out.at[:, :, pl.ds(1, size_x - 2), :, pl.ds(low, 128)]
        pair = (there, tops) if inward else (tops, there)
        return pltpu.make_async_copy(*pair, sems.at[2])

    for side in range(2):
        plane_copy(side, True).start()
    top_copy(True).start()

    near = small[0] + small[1]
    far = small[2] + small[3]
    group = 64
    blocks = []
    lane = lax.broadcasted_iota(jnp.int32, (channels, 128), 1)
    for pair in range(2):
        turned_near = pltpu.roll(near[pair], group, 1)
        turned_far = pltpu.roll(far[pair], group, 1)
        blocks.append(jnp.where(lane < group, near[pair], turned_far))
        blocks.append(jnp.where(lane < group, turned_near, far[pair]))
    trace = near[2] + pltpu.roll(far[2], group, 1)
    mine = blocks[0] - 0.25 * trace
    mine = pltpu.roll(mine, (128 - narrow * 4) % 128, 1)
    boundary[...] = mine[:, :4]
    rows = jnp.concatenate(blocks, axis=1)
    added = jnp.zeros((counted.shape[0], channels), F32)
    for piece in reversed(split3(rows)):
        added = added + lax.dot_general(counted[...], piece, NT, preferred_element_type=F32)
    added = jnp.concatenate([added, jnp.zeros((added.shape[0], 128 - channels), F32)], axis=1)
    at_top = lax.broadcasted_iota(jnp.int32, added.shape, 1) == 127
    size_y = out.shape[3]

    plane_copy(0, True).wait()
    plane_copy(1, True).wait()
    for side in range(2):
        scale = coefficients[0, places[side]].astype(F32) * (1.0 / 12.0)
        for channel in range(channels):
            part, wave = divmod(channel, waves)
            rows_at = pl.ds(channel * size_y, size_y)
            if side == 0:
                value = same_plane[rows_at, :]
                before = same_corner[pl.ds(channel, 1), :]
                after = same_corner[pl.ds(channels + channel, 1), :]
            else:
                value = cross_plane[rows_at, :]
                base = channels * size_y
                before = cross_plane[pl.ds(base + channel, 1), :]
                after = cross_plane[pl.ds(base + channels + channel, 1), :]
            twice = y_sum(value, before, after)
            near_sum = z_sum(twice + 2.0 * value) + 2.0 * twice
            planes[side, part, wave] = planes[side, part, wave] - scale * near_sum

    top_copy(True).wait()
    for channel in range(channels):
        part, wave = divmod(channel, waves)
        lifted = jnp.where(at_top, pltpu.roll(added, 127 - channel, 1), 0.0)
        lifted = lifted.reshape(size_x, size_y, 128)
        tops[part, wave] = tops[part, wave] + lifted[1:last]
        for side, first_end in ((0, True), (1, True)):
            mixed = jnp.where(places[side] == 0, lifted[0], lifted[last])
            planes[side, part, wave, :, pl.ds(low, 128)] = (
                planes[side, part, wave, :, pl.ds(low, 128)] + mixed
            )
    for side in range(2):
        plane_copy(side, False).start()
    top_copy(False).start()
    for side in range(2):
        plane_copy(side, False).wait()
    top_copy(False).wait()


def final(coefficients, same_plane, same_corner, cross_plane, small, counted, started):
    parts, waves, size_x, size_y, size_z = started.shape
    channels = parts * waves
    vmem = pl.BlockSpec(memory_space=pltpu.VMEM)
    anywhere = pl.BlockSpec(memory_space=pl.ANY)
    return pl.pallas_call(
        final_kernel,
        in_specs=[vmem] * 6 + [anywhere],
        out_specs=[anywhere, vmem],
        out_shape=[
            jax.ShapeDtypeStruct(started.shape, F32),
            jax.ShapeDtypeStruct((channels, 4), F32),
        ],
        scratch_shapes=[
            pltpu.VMEM((2, parts, waves, size_y, size_z), F32),
            pltpu.VMEM((parts, waves, size_x - 2, size_y, 128), F32),
            pltpu.SemaphoreType.DMA((3,)),
        ],
        input_output_aliases={6: 0},
        name="final",
    )(coefficients, same_plane, same_corner, cross_plane, small, counted, started)


N_WIDE = 8
N_NARROW = 16
AXES = ("wide", "narrow")


def moved(value, rule):
    pairs = []
    for wide in range(N_WIDE):
        for narrow in range(N_NARROW):
            target = rule(wide, narrow)
            if target is not None and 0 <= target[0] < N_WIDE and 0 <= target[1] < N_NARROW:
                pairs.append((wide * N_NARROW + narrow, target[0] * N_NARROW + target[1]))
    return lax.ppermute(value, AXES, pairs)


def along_y(step):
    return lambda w, n: (w ^ (step >> 1), n ^ ((step & 1) * 8))


def on_device(
    volume_field,
    coefficients,
    density,
    boundary_matrix,
    upsample,
    trace_cell,
    trace_row,
    slot_counts,
):
    parts, waves, size_x, size_y, size_z = volume_field.shape
    channels = parts * waves
    wide = lax.axis_index("wide")
    even = wide % 2 == 0
    last = size_x - 1
    same_x = jnp.where(even, last, 0)
    cross_x = jnp.where(even, 0, last)

    upward = volume_field[:, :, :, size_y - 1]
    downward = volume_field[:, :, :, 0]
    before = moved(upward, lambda w, n: (w, n + 1))
    after = moved(downward, lambda w, n: (w, n - 1))
    same_out = lax.dynamic_index_in_dim(volume_field, same_x, 2, keepdims=False)
    same_out = same_out.reshape(channels * size_y, size_z)
    same_plane = moved(same_out, lambda w, n: (w ^ 1, n))

    top = volume_field[:, :, :, :, size_z - 1].reshape(channels, size_x * size_y)
    bem, trace, counted = front(
        upsample,
        slot_counts,
        density.reshape(channels, density.shape[2]),
        boundary_matrix,
        top,
        trace_cell.reshape(1, -1),
        trace_row.reshape(1, -1),
    )
    blocks = [bem]
    traces = trace[0]
    for step in range(1, 4):
        message = jnp.stack([bem, trace[step]])
        got = moved(message, lambda w, n, s=step: (w ^ (2 * s), n))
        blocks.append(got[0])
        traces = traces + got[1]
    lane = lax.broadcasted_iota(jnp.int32, bem.shape, 1)
    packed = [
        jnp.concatenate([blocks[2 * k][:, :64], blocks[2 * k + 1][:, :64]], axis=1)
        for k in range(2)
    ]
    small = jnp.stack(packed + [traces])
    for step in (2, 4, 1):
        small = small + moved(small, lambda w, n, s=step: (w, n ^ s))

    half = waves // 2
    started = interior(volume_field, coefficients, before, after, 0, half)

    messages = [small] + [moved(small, along_y(step)) for step in range(1, 4)]
    corner_out = jnp.stack(
        [lax.dynamic_index_in_dim(face, same_x, 2, keepdims=False) for face in (before, after)]
    ).reshape(2 * channels, size_z)
    same_corner = moved(corner_out, lambda w, n: (w ^ 1, n))
    cross_out = jnp.concatenate(
        [
            lax.dynamic_index_in_dim(volume_field, cross_x, 2, keepdims=False).reshape(
                channels * size_y, size_z
            )
        ]
        + [
            lax.dynamic_index_in_dim(face, cross_x, 2, keepdims=False).reshape(channels, size_z)
            for face in (before, after)
        ],
        axis=0,
    )
    cross_plane = moved(cross_out, lambda w, n: (w + (1 if w % 2 else -1), n))

    started = interior(
        volume_field, coefficients, before, after, half, waves - half, started
    )
    volume_out, boundary = final(
        coefficients,
        same_plane,
        same_corner,
        cross_plane,
        jnp.stack(messages),
        counted,
        started,
    )
    return volume_out, boundary.reshape(parts, waves, 4)


def solution(mesh):
    return jax.shard_map(
        on_device,
        mesh=mesh,
        in_specs=(
            P(None, None, "wide", "narrow", None),
            P(None, "wide", "narrow", None),
            P(None, None, "narrow"),
            P(None, None, "wide", "narrow"),
            P("narrow"),
            P("wide", "narrow", None),
            P("wide", "narrow", None),
            P("wide", "narrow"),
        ),
        out_specs=(P(None, None, "wide", "narrow", None), P(None, None, ("wide", "narrow"))),
        check_vma=False,
    )
```

```python
from functools import partial

import jax
import jax.numpy as jnp
from jax import lax
from jax.experimental import pallas as pl
from jax.experimental.pallas import tpu as pltpu
from jax.sharding import PartitionSpec as P


UMAX = 4
CALLS = 4
F32 = jnp.float32
BF16 = jnp.bfloat16
NT = (((1,), (1,)), ((), ()))
TN = (((0,), (0,)), ((), ()))


def split3(value):
    high = value.astype(BF16)
    rest = value - high.astype(F32)
    middle = rest.astype(BF16)
    low = (rest - middle.astype(F32)).astype(BF16)
    return high, middle, low


VMEM = pl.BlockSpec(memory_space=pltpu.VMEM)
ANY = pl.BlockSpec(memory_space=pl.ANY)
HBM = pl.BlockSpec(memory_space=pltpu.HBM)
LIMIT = pltpu.CompilerParams(vmem_limit_bytes=30 << 20)
SMEM = pl.BlockSpec(memory_space=pltpu.SMEM)


def near(value):
    return pltpu.with_memory_space_constraint(value, pltpu.VMEM)


def afar(value):
    return pltpu.with_memory_space_constraint(value, pltpu.HBM)


def sides_of(size_x):
    even = lax.axis_index("wide") % 2 == 0
    return jnp.where(even, size_x - 1, 0), jnp.where(even, 0, size_x - 1)


def run_all(copies):
    for copy in copies:
        copy.start()
    for copy in copies:
        copy.wait()


def faces_kernel(volume, upward, downward, same, sems):
    same_x, _ = sides_of(volume.shape[1])
    run_all(
        [
            pltpu.make_async_copy(volume.at[:, :, volume.shape[2] - 1], upward, sems.at[0]),
            pltpu.make_async_copy(volume.at[:, :, 0], downward, sems.at[1]),
            pltpu.make_async_copy(volume.at[:, same_x], same, sems.at[2]),
        ]
    )


def faces(volume):
    channels, size_x, size_y, size_z = volume.shape
    return pl.pallas_call(
        faces_kernel,
        in_specs=[HBM],
        out_specs=[VMEM] * 3,
        out_shape=[
            pltpu.VMEM((channels, size_x, size_z), F32),
            pltpu.VMEM((channels, size_x, size_z), F32),
            pltpu.VMEM((channels, size_y, size_z), F32),
        ],
        scratch_shapes=[pltpu.SemaphoreType.DMA((3,))],
        compiler_params=LIMIT,
        name="faces",
    )(afar(volume))


def pack_kernel(volume, before, after, corner, cross, sems):
    same_x, cross_x = sides_of(volume.shape[1])
    channels = volume.shape[0]
    run_all(
        [
            pltpu.make_async_copy(
                volume.at[:, cross_x], cross.at[pl.ds(0, channels)], sems.at[0]
            ),
            pltpu.make_async_copy(before.at[:, same_x], corner.at[0], sems.at[1]),
            pltpu.make_async_copy(after.at[:, same_x], corner.at[1], sems.at[2]),
            pltpu.make_async_copy(before.at[:, cross_x], cross.at[channels], sems.at[3]),
            pltpu.make_async_copy(after.at[:, cross_x], cross.at[channels + 1], sems.at[4]),
        ]
    )


def pack(volume, before, after):
    channels, _, size_y, size_z = volume.shape
    return pl.pallas_call(
        pack_kernel,
        in_specs=[HBM, VMEM, VMEM],
        out_specs=[VMEM] * 2,
        out_shape=[
            pltpu.VMEM((2, channels, size_z), F32),
            pltpu.VMEM((channels + 2, size_y, size_z), F32),
        ],
        scratch_shapes=[pltpu.SemaphoreType.DMA((5,))],
        compiler_params=LIMIT,
        name="pack",
    )(afar(volume), near(before), near(after))


def front_kernel(
    upsample, counts, volume, density, matrix, cells, rows, own, one, two, three, count_out,
    acc, top, sem,
):
    step = pl.program_id(0)
    steps = pl.num_programs(0)
    wide = lax.axis_index("wide")
    channels, size_x, size_y, size_z = volume.shape
    top_copy = pltpu.make_async_copy(volume.at[:, :, :, pl.ds(size_z - 128, 128)], top, sem)

    @pl.when(step == 0)
    def _():
        top_copy.start()
        acc[...] = jnp.zeros_like(acc)
        slots = cells.shape[1]
        cell_count, row_count = count_out.shape
        live = lax.broadcasted_iota(jnp.int32, (1, slots), 1) < counts[0, 0]
        cell_of = jnp.where(live, cells[...], -1)
        cell_hit = lax.broadcasted_iota(jnp.int32, (cell_count, slots), 0) == cell_of
        row_of = rows[...] ^ (wide * (row_count // 8))
        row_hit = lax.broadcasted_iota(jnp.int32, (row_count, slots), 0) == row_of
        cell_hit = jnp.where(cell_hit, 1.0, 0.0).astype(BF16)
        row_hit = jnp.where(row_hit, 1.0, 0.0).astype(BF16)
        counted = lax.dot_general(cell_hit, row_hit, NT, preferred_element_type=F32)
        count_out[...] = counted.astype(BF16)

    width = density.shape[1] // BLOCKS_A_STEP
    group = matrix.shape[2]
    lane = lax.broadcasted_iota(jnp.int32, (channels, width), 1)
    total = acc[...]
    for block in range(BLOCKS_A_STEP):
        columns = pl.ds(block * width, width)
        here = density[:, columns]
        following = jnp.where(lane == width - 1, here, pltpu.roll(here, width - 1, 1))
        factor = upsample[step * BLOCKS_A_STEP + block]
        inverse = jnp.where(
            factor == 1, 1.0, jnp.where(factor == 2, 0.5, jnp.where(factor == 3, 1.0 / 3.0, 0.25))
        )
        for level in range(UMAX):
            share = jnp.where(level < factor, inverse, 0.0)
            blend = level * inverse
            fine = ((1.0 - blend) * share) * here + (blend * share) * following
            both = matrix[:, level, :, columns].reshape(2 * group, width)
            total = total + lax.dot_general(
                fine.astype(BF16), both, NT, preferred_element_type=F32
            )
    acc[...] = total

    @pl.when(step == steps - 1)
    def _():
        waves = channels // 2
        turned = pltpu.roll(total, group, 1)
        bem = jnp.concatenate(
            [total[:waves] - turned[waves:], total[waves:] + turned[:waves]], axis=0
        )
        top_copy.wait()
        cell_count = size_x * size_y
        at = lax.broadcasted_iota(jnp.int32, (cell_count, 128), 1)
        tops = jnp.zeros((cell_count, 128), F32)
        for channel in range(channels):
            value = top[channel].reshape(cell_count, 128)
            tops = jnp.where(at == channel, pltpu.roll(value, (channel + 1) % 128, 1), tops)
        counted = count_out[...]
        traces = jnp.zeros((128, counted.shape[1]), F32)
        for piece in reversed(split3(tops)):
            traces = traces + lax.dot_general(piece, counted, TN, preferred_element_type=F32)
        for part, target in enumerate((own, one, two, three)):
            target[0] = bem
            target[1] = traces[:channels, part * 128 : (part + 1) * 128]


BLOCKS_A_STEP = 2


def front(upsample, counts, volume, density, matrix, cells, rows):
    blocks = upsample.shape[0]
    channels, columns = density.shape
    width = columns * BLOCKS_A_STEP // blocks
    group = matrix.shape[2]
    slots = cells.shape[1]
    message = pltpu.VMEM((2, channels, 128), F32)
    return pl.pallas_call(
        front_kernel,
        grid=(blocks // BLOCKS_A_STEP,),
        in_specs=[
            SMEM,
            SMEM,
            HBM,
            pl.BlockSpec((channels, width), lambda b: (0, b)),
            pl.BlockSpec((2, UMAX, group, width), lambda b: (0, 0, 0, b)),
            pl.BlockSpec((1, slots), lambda b: (0, 0)),
            pl.BlockSpec((1, slots), lambda b: (0, 0)),
        ],
        out_specs=[VMEM] * 5,
        out_shape=[message] * 4 + [pltpu.VMEM((256, 512), BF16)],
        scratch_shapes=[
            pltpu.VMEM((channels, 128), F32),
            pltpu.VMEM(volume.shape[:3] + (128,), F32),
            pltpu.SemaphoreType.DMA,
        ],
        compiler_params=LIMIT,
        name="front",
    )(upsample, counts, afar(volume), density, matrix, cells, rows)


def join_kernel(own, one, two, three, out):
    group = 64
    lane = lax.broadcasted_iota(jnp.int32, own.shape[1:], 1)
    out[0] = jnp.where(lane < group, own[0], pltpu.roll(one[0], group, 1))
    out[1] = jnp.where(lane < group, two[0], pltpu.roll(three[0], group, 1))
    out[2] = (own[1] + one[1]) + (two[1] + three[1])


def join(own, one, two, three):
    return pl.pallas_call(
        join_kernel,
        in_specs=[VMEM] * 4,
        out_specs=VMEM,
        out_shape=pltpu.VMEM((3,) + own.shape[1:], F32),
        compiler_params=LIMIT,
        name="join",
    )(*[near(value) for value in (own, one, two, three)])


def spread_kernel(own, one, two, three, out):
    group = 64
    lane = lax.broadcasted_iota(jnp.int32, own.shape[1:], 1)
    for pair in range(2):
        close = own[pair] + one[pair]
        distant = two[pair] + three[pair]
        out[2 * pair] = jnp.where(lane < group, close, pltpu.roll(distant, group, 1))
        out[2 * pair + 1] = jnp.where(lane < group, pltpu.roll(close, group, 1), distant)
    out[4] = (own[2] + one[2]) + pltpu.roll(two[2] + three[2], group, 1)


def spread(own, one, two, three):
    return pl.pallas_call(
        spread_kernel,
        in_specs=[VMEM] * 4,
        out_specs=VMEM,
        out_shape=pltpu.VMEM((5,) + own.shape[1:], F32),
        compiler_params=LIMIT,
        name="spread",
    )(*[near(value) for value in (own, one, two, three)])


def y_sum(value, before, after):
    half = value.shape[0] // 2
    low, high = value[:half], value[half:]
    at = lax.broadcasted_iota(jnp.int32, low.shape, 0)
    low_down, high_down = pltpu.roll(low, 1, 0), pltpu.roll(high, 1, 0)
    low_up, high_up = pltpu.roll(low, half - 1, 0), pltpu.roll(high, half - 1, 0)
    first, final_row = at == 0, at == half - 1
    low_sum = jnp.where(first, before, low_down) + jnp.where(final_row, high_up, low_up)
    high_sum = jnp.where(first, low_down, high_down) + jnp.where(final_row, after, high_up)
    return jnp.concatenate([low_sum, high_sum], axis=0)


def z_sum(value):
    tiles = value.shape[1] // 128
    pieces = [value[:, 128 * k : 128 * (k + 1)] for k in range(tiles)]
    at = lax.broadcasted_iota(jnp.int32, pieces[0].shape, 1)
    first, final_lane = at == 0, at == 127
    down = [pltpu.roll(piece, 1, 1) for piece in pieces]
    up = [pltpu.roll(piece, 127, 1) for piece in pieces]
    sums = []
    for k in range(tiles):
        below = down[k - 1] if k > 0 else 0.0
        above = up[k + 1] if k < tiles - 1 else 0.0
        sums.append(jnp.where(first, below, down[k]) + jnp.where(final_lane, above, up[k]))
    return jnp.concatenate(sums, axis=1)


def interior_kernel(volume, coefficients, before, after, *refs, first):
    out, planes, tops, scales, twice, mixed = refs[-6:]
    step = pl.program_id(0)
    _, _, size_x, size_y, size_z = volume.shape
    low = size_z - 128

    @pl.when(step == 0)
    def _():
        def prepare(x, carry):
            scale = coefficients[0, x].astype(F32)
            scales[0, x] = scale * (8.0 / 3.0) - coefficients[1, x].astype(F32)
            scales[1, x] = scale * (1.0 / 12.0)
            scales[2, x] = coefficients[2, x].astype(F32)
            return carry

        lax.fori_loop(0, size_x, prepare, 0)
        nothing = jnp.zeros((size_y, size_z), F32)
        for part in range(2):
            for x in (0, size_x + 1):
                twice[part, x] = nothing
                mixed[part, x] = nothing

    waves = before.shape[0] // 2
    wave = first + step

    def along(x, carry):
        for part in range(2):
            value = volume[part, 0, x]
            channel = part * waves + wave
            row = pl.ds(x, 1)
            total = y_sum(value, before[channel, row, :], after[channel, row, :])
            twice[part, x + 1] = total + total
            mixed[part, x + 1] = total + (value + value)
        return carry

    lax.fori_loop(0, size_x, along, 0)

    def across(x, carry):
        own = []
        for part in range(2):
            level = mixed[part, x] + mixed[part, x + 2] + twice[part, x + 1]
            nearby = z_sum(level) + (twice[part, x] + twice[part, x + 2])
            own.append(nearby)
        real, imag = volume[0, 0, x], volume[1, 0, x]
        diagonal, twelfth, absorb = scales[0, x], scales[1, x], scales[2, x]
        real_out = (diagonal * real - twelfth * own[0]) + absorb * imag
        imag_out = (diagonal * imag - twelfth * own[1]) - absorb * real
        out[0, 0, x] = real_out
        out[1, 0, x] = imag_out
        tops[0, step, x] = real_out[:, low:]
        tops[1, step, x] = imag_out[:, low:]
        return carry

    lax.fori_loop(0, size_x, across, 0)
    for part in range(2):
        planes[0, part, step] = out[part, 0, 0]
        planes[1, part, step] = out[part, 0, size_x - 1]


def interior(volume, coefficients, before, after, first, count, previous=None):
    parts, _, size_x, size_y, size_z = volume.shape
    whole = pl.BlockSpec((parts, 1, size_x, size_y, size_z), lambda i: (0, first + i, 0, 0, 0))
    fixed = pl.BlockSpec(coefficients.shape, lambda i: (0, 0, 0, 0))
    specs = [whole, fixed, VMEM, VMEM]
    operands = [afar(volume), coefficients, near(before), near(after)]
    aliases = {}
    if previous is not None:
        specs.append(ANY)
        operands.append(previous)
        aliases = {4: 0}
    work = pltpu.VMEM((parts, size_x + 2, size_y, size_z), F32)
    return pl.pallas_call(
        partial(interior_kernel, first=first),
        grid=(count,),
        in_specs=specs,
        out_specs=[whole, VMEM, VMEM],
        out_shape=[
            jax.ShapeDtypeStruct(volume.shape, F32),
            pltpu.VMEM((2, parts, count, size_y, size_z), F32),
            pltpu.VMEM((parts, count, size_x, size_y, 128), F32),
        ],
        scratch_shapes=[pltpu.VMEM((3, size_x, size_y, size_z), F32), work, work],
        input_output_aliases=aliases,
        compiler_params=LIMIT,
        name="interior",
    )(*operands)


def final_kernel(coefficients, same_plane, same_corner, cross_plane, small, counted, *refs):
    edges = refs[: 2 * CALLS]
    out, boundary, planes, tops, scales, sems, scale_sems = refs[2 * CALLS + 1 :]
    narrow = lax.axis_index("narrow")
    channels, size_x, size_y, size_z = out.shape
    places = sides_of(size_x)
    last = size_x - 1
    low = size_z - 128
    waves = channels // 2
    scale_copies = [
        pltpu.make_async_copy(coefficients.at[0, places[side]], scales.at[side], scale_sems.at[side])
        for side in range(2)
    ]
    for copy in scale_copies:
        copy.start()

    mine = pltpu.roll(small[0] - 0.25 * small[4], (128 - narrow * 4) % 128, 1)
    mine = mine.T
    boundary[0] = mine[:4, :waves]
    boundary[1] = mine[:4, waves:]
    rows = jnp.concatenate([small[k] for k in range(4)], axis=1)
    added = jnp.zeros((counted.shape[0], channels), F32)
    for piece in reversed(split3(rows)):
        added = added + lax.dot_general(counted[...], piece, NT, preferred_element_type=F32)
    added = jnp.concatenate([added, jnp.zeros((added.shape[0], 128 - channels), F32)], axis=1)
    at_top = lax.broadcasted_iota(jnp.int32, added.shape, 1) == 127
    for copy in scale_copies:
        copy.wait()

    copies = []
    count = waves // CALLS
    even = places[1] == 0
    for channel in range(channels):
        part, wave = divmod(channel, waves)
        source, source_top = edges[2 * (wave // count)], edges[2 * (wave // count) + 1]
        wave = wave % count
        lifted = jnp.where(at_top, pltpu.roll(added, 127 - channel, 1), 0.0)
        lifted = lifted.reshape(size_x, size_y, 128)
        for side in range(2):
            scale = scales[side].astype(F32) * (1.0 / 12.0)
            if side == 0:
                value = same_plane[channel]
                ends = [same_corner[k, pl.ds(channel, 1), :] for k in range(2)]
                begun = source[jnp.where(even, 1, 0), part, wave]
                raised = jnp.where(even, lifted[last], lifted[0])
            else:
                value = cross_plane[channel]
                ends = [cross_plane[channels + k, pl.ds(channel, 1), :] for k in range(2)]
                begun = source[jnp.where(even, 0, 1), part, wave]
                raised = jnp.where(even, lifted[0], lifted[last])
            total = y_sum(value, *ends)
            total2 = total + total
            nearby = z_sum(total + (value + value)) + total2
            result = begun - scale * nearby
            planes[side, channel, :, pl.ds(0, low)] = result[:, :low]
            planes[side, channel, :, pl.ds(low, 128)] = result[:, low:] + raised
            copy = pltpu.make_async_copy(
                planes.at[side, channel], out.at[channel, places[side]], sems.at[side, channel]
            )
            copy.start()
            copies.append(copy)
        tops[channel] = source_top[part, wave, pl.ds(1, size_x - 2)] + lifted[1:last]
        copy = pltpu.make_async_copy(
            tops.at[channel],
            out.at[channel, pl.ds(1, size_x - 2), :, pl.ds(low, 128)],
            sems.at[2, channel],
        )
        copy.start()
        copies.append(copy)
    for copy in copies:
        copy.wait()


def final(coefficients, wide_faces, small, counted, edges, started):
    channels, size_x, size_y, size_z = started.shape
    close = [near(v) for v in wide_faces + (small, counted) + tuple(edges)]
    return pl.pallas_call(
        final_kernel,
        in_specs=[HBM] + [VMEM] * len(close) + [ANY],
        out_specs=[ANY, VMEM],
        out_shape=[
            jax.ShapeDtypeStruct(started.shape, F32),
            jax.ShapeDtypeStruct((2, 4, channels // 2), F32),
        ],
        scratch_shapes=[
            pltpu.VMEM((2, channels, size_y, size_z), F32),
            pltpu.VMEM((channels, size_x - 2, size_y, 128), F32),
            pltpu.VMEM((2, size_y, size_z), BF16),
            pltpu.SemaphoreType.DMA((3, channels)),
            pltpu.SemaphoreType.DMA((2,)),
        ],
        input_output_aliases={len(close) + 1: 0},
        compiler_params=LIMIT,
        name="final",
    )(afar(coefficients), *close, started)


N_WIDE = 8
N_NARROW = 16
AXES = ("wide", "narrow")


def moved(value, rule):
    pairs = []
    for wide in range(N_WIDE):
        for narrow in range(N_NARROW):
            target = rule(wide, narrow)
            if target is not None and 0 <= target[0] < N_WIDE and 0 <= target[1] < N_NARROW:
                pairs.append((wide * N_NARROW + narrow, target[0] * N_NARROW + target[1]))
    return lax.ppermute(value, AXES, pairs)


def along_y(step):
    return lambda w, n: (w ^ (step >> 1), n ^ ((step & 1) * 8))


def on_device(
    volume_field,
    coefficients,
    density,
    boundary_matrix,
    upsample,
    trace_cell,
    trace_row,
    slot_counts,
):
    parts, waves, size_x, size_y, size_z = volume_field.shape
    channels = parts * waves
    volume = volume_field.reshape(channels, size_x, size_y, size_z)

    upward, downward, same_out = faces(volume)
    before = moved(upward, lambda w, n: (w, n + 1))
    after = moved(downward, lambda w, n: (w, n - 1))
    same_plane = moved(same_out, lambda w, n: (w ^ 1, n))

    own, one, two, three, counted = front(
        upsample,
        slot_counts,
        volume,
        density.reshape(channels, density.shape[2]),
        boundary_matrix,
        trace_cell.reshape(1, -1),
        trace_row.reshape(1, -1),
    )
    got = [
        moved(message, lambda w, n, s=step: (w ^ (2 * s), n))
        for step, message in ((1, one), (2, two), (3, three))
    ]
    corner_out, cross_out = pack(volume, before, after)
    small = join(own, *got)

    count = waves // CALLS
    started, edges = None, []

    def some_waves(call, started):
        return interior(
            volume_field, coefficients, before, after, call * count, count, started
        )

    started, *more = some_waves(0, started)
    edges += more
    got = [moved(small, along_y(step)) for step in range(1, 4)]
    same_corner = moved(corner_out, lambda w, n: (w ^ 1, n))
    cross_plane = moved(cross_out, lambda w, n: (w + (1 if w % 2 else -1), n))
    small = spread(small, *got)
    for call, step in enumerate((2, 4, 1)):
        started, *more = some_waves(call + 1, started)
        edges += more
        small = small + moved(small, lambda w, n, s=step: (w, n ^ s))

    volume_out, boundary = final(
        coefficients,
        (same_plane, same_corner, cross_plane),
        small,
        counted,
        edges,
        started.reshape(volume.shape),
    )
    return volume_out.reshape(volume_field.shape), boundary.transpose(0, 2, 1)


def solution(mesh):
    return jax.shard_map(
        on_device,
        mesh=mesh,
        in_specs=(
            P(None, None, "wide", "narrow", None),
            P(None, "wide", "narrow", None),
            P(None, None, "narrow"),
            P(None, None, "wide", "narrow"),
            P("narrow"),
            P("wide", "narrow", None),
            P("wide", "narrow", None),
            P("wide", "narrow"),
        ),
        out_specs=(P(None, None, "wide", "narrow", None), P(None, None, ("wide", "narrow"))),
        check_vma=False,
    )
```

```python
from functools import partial

import jax
import jax.numpy as jnp
from jax import lax
from jax.experimental import pallas as pl
from jax.experimental.pallas import tpu as pltpu
from jax.sharding import PartitionSpec as P


UMAX = 4
CALLS = 4
F32 = jnp.float32
BF16 = jnp.bfloat16
NT = (((1,), (1,)), ((), ()))
TN = (((0,), (0,)), ((), ()))


def split3(value):
    high = value.astype(BF16)
    rest = value - high.astype(F32)
    middle = rest.astype(BF16)
    low = (rest - middle.astype(F32)).astype(BF16)
    return high, middle, low


VMEM = pl.BlockSpec(memory_space=pltpu.VMEM)
ANY = pl.BlockSpec(memory_space=pl.ANY)
HBM = pl.BlockSpec(memory_space=pltpu.HBM)
LIMIT = pltpu.CompilerParams(vmem_limit_bytes=30 << 20)
SMEM = pl.BlockSpec(memory_space=pltpu.SMEM)


def near(value):
    return pltpu.with_memory_space_constraint(value, pltpu.VMEM)


def afar(value):
    return pltpu.with_memory_space_constraint(value, pltpu.HBM)


def sides_of(size_x):
    even = lax.axis_index("wide") % 2 == 0
    return jnp.where(even, size_x - 1, 0), jnp.where(even, 0, size_x - 1)


def run_all(copies):
    for copy in copies:
        copy.start()
    for copy in copies:
        copy.wait()


def faces_kernel(volume, upward, downward, same, cross, sems):
    channels, size_x, size_y, _ = volume.shape
    same_x, cross_x = sides_of(size_x)
    run_all(
        [
            pltpu.make_async_copy(volume.at[:, :, size_y - 1], upward, sems.at[0]),
            pltpu.make_async_copy(volume.at[:, :, 0], downward, sems.at[1]),
            pltpu.make_async_copy(volume.at[:, same_x], same, sems.at[2]),
            pltpu.make_async_copy(volume.at[:, cross_x], cross.at[pl.ds(0, channels)], sems.at[3]),
        ]
    )


def faces(volume):
    channels, size_x, size_y, size_z = volume.shape
    return pl.pallas_call(
        faces_kernel,
        in_specs=[HBM],
        out_specs=[VMEM] * 4,
        out_shape=[
            pltpu.VMEM((channels, size_x, size_z), F32),
            pltpu.VMEM((channels, size_x, size_z), F32),
            pltpu.VMEM((channels, size_y, size_z), F32),
            pltpu.VMEM((channels + 2, size_y, size_z), F32),
        ],
        scratch_shapes=[pltpu.SemaphoreType.DMA((4,))],
        compiler_params=LIMIT,
        name="faces",
    )(afar(volume))


def front_kernel(
    upsample, counts, volume, cells, rows, density_far, matrix_far,
    own, one, two, three, count_out, density, matrix, sems,
):
    wide = lax.axis_index("wide")
    density_copy = pltpu.make_async_copy(density_far, density, sems.at[UMAX])
    density_copy.start()
    level_copies = [
        pltpu.make_async_copy(matrix_far.at[:, level], matrix.at[level], sems.at[level])
        for level in range(UMAX)
    ]
    for copy in level_copies:
        copy.start()
    channels, _, _, size_z = volume.shape
    slots = cells.shape[1]
    cell_count, row_count = count_out.shape
    live = lax.broadcasted_iota(jnp.int32, (1, slots), 1) < counts[0, 0]
    cell_of = jnp.where(live, cells[...], -1)
    cell_hit = lax.broadcasted_iota(jnp.int32, (cell_count, slots), 0) == cell_of
    row_of = rows[...] ^ (wide * (row_count // 8))
    row_hit = lax.broadcasted_iota(jnp.int32, (row_count, slots), 0) == row_of
    cell_hit = jnp.where(cell_hit, 1.0, 0.0).astype(BF16)
    row_hit = jnp.where(row_hit, 1.0, 0.0).astype(BF16)
    counted = lax.dot_general(cell_hit, row_hit, NT, preferred_element_type=F32).astype(BF16)
    count_out[...] = counted

    at = lax.broadcasted_iota(jnp.int32, (cell_count, 128), 1)
    tops = jnp.zeros((cell_count, 128), F32)
    for channel in range(channels):
        value = volume[channel, :, :, pl.ds(size_z - 128, 128)].reshape(cell_count, 128)
        tops = jnp.where(at == channel, pltpu.roll(value, (channel + 1) % 128, 1), tops)
    traces = jnp.zeros((128, row_count), F32)
    for piece in reversed(split3(tops)):
        traces = traces + lax.dot_general(piece, counted, TN, preferred_element_type=F32)
    blocks = upsample.shape[0]
    width = density.shape[1] // blocks
    group = matrix.shape[2]
    lane = lax.broadcasted_iota(jnp.int32, (channels, width), 1)
    total = jnp.zeros((channels, 2 * group), F32)
    density_copy.wait()
    pairs = []
    for block in range(blocks):
        here = density[:, pl.ds(block * width, width)]
        factor = upsample[block]
        inverse = jnp.where(
            factor == 1, 1.0, jnp.where(factor == 2, 0.5, jnp.where(factor == 3, 1.0 / 3.0, 0.25))
        )
        pairs.append((here, factor, inverse))
    for level in range(UMAX):
        level_copies[level].wait()
        for block, (here, factor, inverse) in enumerate(pairs):
            following = jnp.where(lane == width - 1, here, pltpu.roll(here, width - 1, 1))
            share = jnp.where(level < factor, inverse, 0.0)
            blend = level * inverse
            fine = ((1.0 - blend) * share) * here + (blend * share) * following
            both = matrix[level, :, :, pl.ds(block * width, width)].reshape(2 * group, width)
            total = total + lax.dot_general(
                fine.astype(BF16), both, NT, preferred_element_type=F32
            )

    waves = channels // 2
    turned = pltpu.roll(total, group, 1)
    bem = jnp.concatenate(
        [total[:waves] - turned[waves:], total[waves:] + turned[:waves]], axis=0
    )
    for part, target in enumerate((own, one, two, three)):
        target[0] = bem
        target[1] = traces[:channels, part * 128 : (part + 1) * 128]


def front(upsample, counts, volume, density, matrix, cells, rows):
    channels = density.shape[0]
    message = pltpu.VMEM((2, channels, 128), F32)
    return pl.pallas_call(
        front_kernel,
        in_specs=[SMEM, SMEM] + [VMEM] * 3 + [HBM] * 2,
        out_specs=[VMEM] * 5,
        out_shape=[message] * 4 + [pltpu.VMEM((256, 512), BF16)],
        scratch_shapes=[
            pltpu.VMEM(density.shape, F32),
            pltpu.VMEM((UMAX, 2) + matrix.shape[2:], BF16),
            pltpu.SemaphoreType.DMA((UMAX + 1,)),
        ],
        compiler_params=LIMIT,
        name="front",
    )(upsample, counts, near(volume), near(cells), near(rows), afar(density), afar(matrix))


def join_kernel(own, one, two, three, before, after, cross_in, out, corner, cross, sems):
    group = 64
    channels, size_x, size_z = before.shape
    same_x, cross_x = sides_of(size_x)
    copies = [
        pltpu.make_async_copy(face.at[:, cross_x], cross.at[channels + k], sems.at[k])
        for k, face in enumerate((before, after))
    ]
    for copy in copies:
        copy.start()
    lane = lax.broadcasted_iota(jnp.int32, own.shape[1:], 1)
    sums = (
        jnp.where(lane < group, own[0], pltpu.roll(one[0], group, 1)),
        jnp.where(lane < group, two[0], pltpu.roll(three[0], group, 1)),
        (own[1] + one[1]) + (two[1] + three[1]),
    )
    for k in range(3):
        out[k] = sums[k]
        corner[k] = sums[k]
    for channel in range(channels):
        for k, face in enumerate((before, after)):
            row = face[channel, pl.ds(same_x, 1), :]
            for tile in range(size_z // 128):
                corner[3 + 4 * k + tile, pl.ds(channel, 1), :] = row[
                    :, 128 * tile : 128 * (tile + 1)
                ]
    for copy in copies:
        copy.wait()


def join(own, one, two, three, before, after, cross):
    channels = before.shape[0]
    operands = [near(v) for v in (own, one, two, three, before, after, cross)]
    return pl.pallas_call(
        join_kernel,
        in_specs=[VMEM] * 7,
        out_specs=[VMEM] * 3,
        out_shape=[
            pltpu.VMEM((3, channels, 128), F32),
            pltpu.VMEM((11, channels, 128), F32),
            pltpu.VMEM(cross.shape, F32),
        ],
        scratch_shapes=[pltpu.SemaphoreType.DMA((2,))],
        input_output_aliases={6: 2},
        compiler_params=LIMIT,
        name="join",
    )(*operands)


def spread_kernel(own, one, two, three, out):
    group = 64
    lane = lax.broadcasted_iota(jnp.int32, own.shape[1:], 1)
    for pair in range(2):
        close = own[pair] + one[pair]
        distant = two[pair] + three[pair]
        out[2 * pair] = jnp.where(lane < group, close, pltpu.roll(distant, group, 1))
        out[2 * pair + 1] = jnp.where(lane < group, pltpu.roll(close, group, 1), distant)
    out[4] = (own[2] + one[2]) + pltpu.roll(two[2] + three[2], group, 1)


def spread(own, one, two, three):
    return pl.pallas_call(
        spread_kernel,
        in_specs=[VMEM] * 4,
        out_specs=VMEM,
        out_shape=pltpu.VMEM((5,) + own.shape[1:], F32),
        compiler_params=LIMIT,
        name="spread",
    )(*[near(value) for value in (own, one, two, three)])


def y_sum(value, before, after):
    half = value.shape[0] // 2
    low, high = value[:half], value[half:]
    at = lax.broadcasted_iota(jnp.int32, low.shape, 0)
    low_down, high_down = pltpu.roll(low, 1, 0), pltpu.roll(high, 1, 0)
    low_up, high_up = pltpu.roll(low, half - 1, 0), pltpu.roll(high, half - 1, 0)
    first, final_row = at == 0, at == half - 1
    low_sum = jnp.where(first, before, low_down) + jnp.where(final_row, high_up, low_up)
    high_sum = jnp.where(first, low_down, high_down) + jnp.where(final_row, after, high_up)
    return jnp.concatenate([low_sum, high_sum], axis=0)


def z_sum(value):
    tiles = value.shape[1] // 128
    pieces = [value[:, 128 * k : 128 * (k + 1)] for k in range(tiles)]
    at = lax.broadcasted_iota(jnp.int32, pieces[0].shape, 1)
    first, final_lane = at == 0, at == 127
    down = [pltpu.roll(piece, 1, 1) for piece in pieces]
    up = [pltpu.roll(piece, 127, 1) for piece in pieces]
    sums = []
    for k in range(tiles):
        below = down[k - 1] if k > 0 else 0.0
        above = up[k + 1] if k < tiles - 1 else 0.0
        sums.append(jnp.where(first, below, down[k]) + jnp.where(final_lane, above, up[k]))
    return jnp.concatenate(sums, axis=1)


PLANES = 4


def interior_kernel(volume, given, before, after, *refs, first, prepares):
    if prepares:
        out, planes, tops, scales, buffers, sums, mixed, sems = refs
    else:
        _, out, planes, tops, buffers, sums, mixed, sems = refs
        scales = given
    parts, count, size_x, size_y, size_z = buffers.shape
    low = size_z - 128
    waves = volume.shape[1]

    if prepares:

        def prepare(x, carry):
            scale = given[0, x].astype(F32)
            scales[0, x] = scale * (8.0 / 3.0) - given[1, x].astype(F32)
            scales[1, x] = scale * (1.0 / 6.0)
            scales[2, x] = given[2, x].astype(F32)
            return carry

        lax.fori_loop(0, size_x, prepare, 0)
    nothing = jnp.zeros((size_y, size_z), F32)
    for part in range(parts):
        for x in (0, size_x + 1):
            sums[part, x] = nothing
            mixed[part, x] = nothing

    for step in range(count):
        wave = first + step

        def along(group, carry):
            for x in [group * PLANES + k for k in range(PLANES)]:
                for part in range(parts):
                    value = volume[part, wave, x]
                    channel = part * waves + wave
                    row = pl.ds(x, 1)
                    total = y_sum(value, before[channel, row, :], after[channel, row, :])
                    sums[part, x + 1] = total
                    mixed[part, x + 1] = 0.5 * total + value
            return carry

        def across(group, carry):
            for x in [group * PLANES + k for k in range(PLANES)]:
                own = []
                for part in range(parts):
                    level = (mixed[part, x] + mixed[part, x + 2]) + sums[part, x + 1]
                    own.append(z_sum(level) + (sums[part, x] + sums[part, x + 2]))
                real, imag = volume[0, wave, x], volume[1, wave, x]
                diagonal, sixth, absorb = scales[0, x], scales[1, x], scales[2, x]
                real_out = (diagonal * real - sixth * own[0]) + absorb * imag
                imag_out = (diagonal * imag - sixth * own[1]) - absorb * real
                for part, result in enumerate((real_out, imag_out)):
                    buffers[part, step, x] = result
                    tops[part, step, x] = result[:, low:]
            some = pl.ds(group * PLANES, PLANES)
            for part in range(parts):
                pltpu.make_async_copy(
                    buffers.at[part, step, some], out.at[part, wave, some], sems.at[part, step]
                ).start()
            return carry

        lax.fori_loop(0, size_x // PLANES, along, 0)
        lax.fori_loop(0, size_x // PLANES, across, 0)
        for part in range(parts):
            planes[0, part, step] = buffers[part, step, 0]
            planes[1, part, step] = buffers[part, step, size_x - 1]
    for step in range(count):
        for part in range(parts):
            pltpu.make_async_copy(
                buffers.at[part, step], out.at[part, first + step], sems.at[part, step]
            ).wait()


def interior(volume, given, before, after, first, count, previous=None):
    parts, _, size_x, size_y, size_z = volume.shape
    prepares = previous is None
    operands = [near(value) for value in (volume, given, before, after)]
    specs = [VMEM] * 4
    aliases = {}
    results = [
        jax.ShapeDtypeStruct(volume.shape, F32),
        pltpu.VMEM((2, parts, count, size_y, size_z), F32),
        pltpu.VMEM((parts, count, size_x, size_y, 128), F32),
    ]
    if prepares:
        results.append(pltpu.VMEM((3, size_x, size_y, size_z), F32))
    else:
        specs.append(ANY)
        operands.append(previous)
        aliases = {4: 0}
    work = pltpu.VMEM((parts, size_x + 2, size_y, size_z), F32)
    return pl.pallas_call(
        partial(interior_kernel, first=first, prepares=prepares),
        in_specs=specs,
        out_specs=[ANY] + [VMEM] * (len(results) - 1),
        out_shape=results,
        scratch_shapes=[
            pltpu.VMEM((parts, count, size_x, size_y, size_z), F32),
            work,
            work,
            pltpu.SemaphoreType.DMA((parts, count)),
        ],
        input_output_aliases=aliases,
        compiler_params=LIMIT,
        name="interior",
    )(*operands)


def final_kernel(scales, same_plane, same_corner, cross_plane, small, counted, *refs):
    edges = refs[: 2 * CALLS]
    out, boundary, planes, tops, sems = refs[2 * CALLS + 1 :]
    narrow = lax.axis_index("narrow")
    channels, size_x, size_y, size_z = out.shape
    places = sides_of(size_x)
    last = size_x - 1
    low = size_z - 128
    waves = channels // 2
    mine = pltpu.roll(small[0] - 0.25 * small[4], (128 - narrow * 4) % 128, 1)
    mine = mine.T
    boundary[0] = mine[:4, :waves]
    boundary[1] = mine[:4, waves:]
    rows = jnp.concatenate([small[k] for k in range(4)], axis=1)
    added = jnp.zeros((counted.shape[0], channels), F32)
    for piece in reversed(split3(rows)):
        added = added + lax.dot_general(counted[...], piece, NT, preferred_element_type=F32)
    added = jnp.concatenate([added, jnp.zeros((added.shape[0], 128 - channels), F32)], axis=1)
    at_top = lax.broadcasted_iota(jnp.int32, added.shape, 1) == 127
    copies = []
    count = waves // CALLS
    even = places[1] == 0
    for channel in range(channels):
        part, wave = divmod(channel, waves)
        source, source_top = edges[2 * (wave // count)], edges[2 * (wave // count) + 1]
        wave = wave % count
        lifted = jnp.where(at_top, pltpu.roll(added, 127 - channel, 1), 0.0)
        lifted = lifted.reshape(size_x, size_y, 128)
        for side in range(2):
            scale = 0.5 * scales[1, places[side]]
            if side == 0:
                value = same_plane[channel]
                ends = [
                    jnp.concatenate(
                        [
                            same_corner[3 + 4 * k + tile, pl.ds(channel, 1), :]
                            for tile in range(size_z // 128)
                        ],
                        axis=1,
                    )
                    for k in range(2)
                ]
                begun = source[jnp.where(even, 1, 0), part, wave]
                raised = jnp.where(even, lifted[last], lifted[0])
            else:
                value = cross_plane[channel]
                ends = [cross_plane[channels + k, pl.ds(channel, 1), :] for k in range(2)]
                begun = source[jnp.where(even, 0, 1), part, wave]
                raised = jnp.where(even, lifted[0], lifted[last])
            total = y_sum(value, *ends)
            total2 = total + total
            nearby = z_sum(total + (value + value)) + total2
            result = begun - scale * nearby
            planes[side, channel, :, pl.ds(0, low)] = result[:, :low]
            planes[side, channel, :, pl.ds(low, 128)] = result[:, low:] + raised
            copy = pltpu.make_async_copy(
                planes.at[side, channel], out.at[channel, places[side]], sems.at[side, channel]
            )
            copy.start()
            copies.append(copy)
        tops[channel] = source_top[part, wave, pl.ds(1, size_x - 2)] + lifted[1:last]
        copy = pltpu.make_async_copy(
            tops.at[channel],
            out.at[channel, pl.ds(1, size_x - 2), :, pl.ds(low, 128)],
            sems.at[2, channel],
        )
        copy.start()
        copies.append(copy)
    for copy in copies:
        copy.wait()


def final(scales, wide_faces, small, counted, edges, started):
    channels, size_x, size_y, size_z = started.shape
    close = [near(v) for v in (scales,) + wide_faces + (small, counted) + tuple(edges)]
    return pl.pallas_call(
        final_kernel,
        in_specs=[VMEM] * len(close) + [ANY],
        out_specs=[ANY, VMEM],
        out_shape=[
            jax.ShapeDtypeStruct(started.shape, F32),
            jax.ShapeDtypeStruct((2, 4, channels // 2), F32),
        ],
        scratch_shapes=[
            pltpu.VMEM((2, channels, size_y, size_z), F32),
            pltpu.VMEM((channels, size_x - 2, size_y, 128), F32),
            pltpu.SemaphoreType.DMA((3, channels)),
        ],
        input_output_aliases={len(close): 0},
        compiler_params=LIMIT,
        name="final",
    )(*close, started)


N_WIDE = 8
N_NARROW = 16
AXES = ("wide", "narrow")


def moved(value, rule):
    pairs = []
    for wide in range(N_WIDE):
        for narrow in range(N_NARROW):
            target = rule(wide, narrow)
            if target is not None and 0 <= target[0] < N_WIDE and 0 <= target[1] < N_NARROW:
                pairs.append((wide * N_NARROW + narrow, target[0] * N_NARROW + target[1]))
    return lax.ppermute(value, AXES, pairs)


def along_y(step):
    return lambda w, n: (w ^ (step >> 1), n ^ ((step & 1) * 8))


def on_device(
    volume_field,
    coefficients,
    density,
    boundary_matrix,
    upsample,
    trace_cell,
    trace_row,
    slot_counts,
):
    parts, waves, size_x, size_y, size_z = volume_field.shape
    channels = parts * waves
    volume = volume_field.reshape(channels, size_x, size_y, size_z)

    upward, downward, same_out, cross_out = faces(volume)
    before = moved(upward, lambda w, n: (w, n + 1))
    after = moved(downward, lambda w, n: (w, n - 1))
    same_plane = moved(same_out, lambda w, n: (w ^ 1, n))

    own, one, two, three, counted = front(
        upsample,
        slot_counts,
        volume,
        density.reshape(channels, density.shape[2]),
        boundary_matrix,
        trace_cell.reshape(1, -1),
        trace_row.reshape(1, -1),
    )
    got = [
        moved(message, lambda w, n, s=step: (w ^ (2 * s), n))
        for step, message in ((1, one), (2, two), (3, three))
    ]
    small, small_corner, cross_out = join(own, *got, before, after, cross_out)

    count = waves // CALLS
    edges = []
    started, *more, scales = interior(volume_field, coefficients, before, after, 0, count)
    edges += more

    def some_waves(call, started):
        return interior(volume_field, scales, before, after, call * count, count, started)

    got = [
        moved(message, along_y(step))
        for step, message in ((1, small), (2, small_corner), (3, small))
    ]
    same_corner = got[1]
    cross_plane = moved(cross_out, lambda w, n: (w + (1 if w % 2 else -1), n))
    small = spread(small, *got)
    for call, step in enumerate((2, 4, 1)):
        started, *more = some_waves(call + 1, started)
        edges += more
        small = small + moved(small, lambda w, n, s=step: (w, n ^ s))

    volume_out, boundary = final(
        scales,
        (same_plane, same_corner, cross_plane),
        small,
        counted,
        edges,
        started.reshape(volume.shape),
    )
    return volume_out.reshape(volume_field.shape), boundary.transpose(0, 2, 1)


def solution(mesh):
    return jax.shard_map(
        on_device,
        mesh=mesh,
        in_specs=(
            P(None, None, "wide", "narrow", None),
            P(None, "wide", "narrow", None),
            P(None, None, "narrow"),
            P(None, None, "wide", "narrow"),
            P("narrow"),
            P("wide", "narrow", None),
            P("wide", "narrow", None),
            P("wide", "narrow"),
        ),
        out_specs=(P(None, None, "wide", "narrow", None), P(None, None, ("wide", "narrow"))),
        check_vma=False,
    )
```

```python
from functools import partial

import jax
import jax.numpy as jnp
from jax import lax
from jax.experimental import pallas as pl
from jax.experimental.pallas import tpu as pltpu
from jax.sharding import PartitionSpec as P


UMAX = 4
CALLS = 4
F32 = jnp.float32
BF16 = jnp.bfloat16
NT = (((1,), (1,)), ((), ()))
NN = (((1,), (0,)), ((), ()))


def split3(value):
    high = value.astype(BF16)
    rest = value - high.astype(F32)
    middle = rest.astype(BF16)
    low = (rest - middle.astype(F32)).astype(BF16)
    return high, middle, low


def three_rows(value):
    return jnp.concatenate(split3(value), axis=0)


def sum_of_three(value):
    size = value.shape[0] // 3
    return (value[2 * size :] + value[size : 2 * size]) + value[:size]


VMEM = pl.BlockSpec(memory_space=pltpu.VMEM)
ANY = pl.BlockSpec(memory_space=pl.ANY)
HBM = pl.BlockSpec(memory_space=pltpu.HBM)
LIMIT = pltpu.CompilerParams(vmem_limit_bytes=30 << 20)
SMEM = pl.BlockSpec(memory_space=pltpu.SMEM)


def near(value):
    return pltpu.with_memory_space_constraint(value, pltpu.VMEM)


def afar(value):
    return pltpu.with_memory_space_constraint(value, pltpu.HBM)


def sides_of(size_x):
    even = lax.axis_index("wide") % 2 == 0
    return jnp.where(even, size_x - 1, 0), jnp.where(even, 0, size_x - 1)


def run_all(copies):
    for copy in copies:
        copy.start()
    for copy in copies:
        copy.wait()


def faces_kernel(volume, upward, downward, same, cross, sems):
    channels, size_x, size_y, _ = volume.shape
    same_x, cross_x = sides_of(size_x)
    run_all(
        [
            pltpu.make_async_copy(volume.at[:, :, size_y - 1], upward, sems.at[0]),
            pltpu.make_async_copy(volume.at[:, :, 0], downward, sems.at[1]),
            pltpu.make_async_copy(volume.at[:, same_x], same, sems.at[2]),
            pltpu.make_async_copy(volume.at[:, cross_x], cross.at[pl.ds(0, channels)], sems.at[3]),
        ]
    )


def faces(volume):
    channels, size_x, size_y, size_z = volume.shape
    return pl.pallas_call(
        faces_kernel,
        in_specs=[HBM],
        out_specs=[VMEM] * 4,
        out_shape=[
            pltpu.VMEM((channels, size_x, size_z), F32),
            pltpu.VMEM((channels, size_x, size_z), F32),
            pltpu.VMEM((channels, size_y, size_z), F32),
            pltpu.VMEM((channels + 2, size_y, size_z), F32),
        ],
        scratch_shapes=[pltpu.SemaphoreType.DMA((4,))],
        compiler_params=LIMIT,
        name="faces",
    )(afar(volume))


def front_kernel(
    upsample, counts, volume, cells, rows, density_far, matrix_far,
    own, one, two, three, count_out, density, matrix, sems,
):
    wide = lax.axis_index("wide")
    density_copy = pltpu.make_async_copy(density_far, density, sems.at[UMAX])
    density_copy.start()
    level_copies = [
        pltpu.make_async_copy(matrix_far.at[:, level], matrix.at[level], sems.at[level])
        for level in range(UMAX)
    ]
    for copy in level_copies:
        copy.start()
    channels, _, _, size_z = volume.shape
    slots = cells.shape[1]
    cell_count, row_count = count_out.shape
    live = lax.broadcasted_iota(jnp.int32, (1, slots), 1) < counts[0, 0]
    cell_of = jnp.where(live, cells[...], -1)
    cell_hit = lax.broadcasted_iota(jnp.int32, (cell_count, slots), 0) == cell_of
    row_of = (rows[...] ^ (wide * (row_count // 8))).astype(F32)
    row_of = jnp.broadcast_to(row_of, (8, slots)).T[:, :1]
    row_hit = lax.broadcasted_iota(jnp.int32, (slots, row_count), 1).astype(F32) == row_of
    cell_hit = jnp.where(cell_hit, 1.0, 0.0).astype(BF16)
    row_hit = jnp.where(row_hit, 1.0, 0.0).astype(BF16)
    counted = lax.dot_general(cell_hit, row_hit, NN, preferred_element_type=F32).astype(BF16)
    count_out[...] = counted

    at = lax.broadcasted_iota(jnp.int32, (cell_count, 128), 1)
    tops = jnp.zeros((cell_count, 128), F32)
    for channel in range(channels):
        value = volume[channel, :, :, pl.ds(size_z - 128, 128)].reshape(cell_count, 128)
        tops = jnp.where(at == channel, pltpu.roll(value, (channel + 1) % 128, 1), tops)
    traces = sum_of_three(
        lax.dot_general(
            three_rows(tops.T[:channels]), counted, NN, preferred_element_type=F32
        )
    )

    blocks = upsample.shape[0]
    width = density.shape[1] // blocks
    group = matrix.shape[2]
    lane = lax.broadcasted_iota(jnp.int32, (channels, width), 1)
    total = jnp.zeros((channels, 2 * group), F32)
    density_copy.wait()
    pairs = []
    for block in range(blocks):
        here = density[:, pl.ds(block * width, width)]
        following = jnp.where(lane == width - 1, here, pltpu.roll(here, width - 1, 1))
        factor = upsample[block]
        inverse = jnp.where(
            factor == 1, 1.0, jnp.where(factor == 2, 0.5, jnp.where(factor == 3, 1.0 / 3.0, 0.25))
        )
        pairs.append((here, following, factor, inverse))
    for level in range(UMAX):
        pieces = []
        for here, following, factor, inverse in pairs:
            share = jnp.where(level < factor, inverse, 0.0)
            blend = level * inverse
            fine = ((1.0 - blend) * share) * here + (blend * share) * following
            pieces.append(fine.astype(BF16))
        level_copies[level].wait()
        both = matrix[level].reshape(2 * group, matrix.shape[3])
        total = total + lax.dot_general(
            jnp.concatenate(pieces, axis=1), both, NT, preferred_element_type=F32
        )

    waves = channels // 2
    turned = pltpu.roll(total, group, 1)
    bem = jnp.concatenate(
        [total[:waves] - turned[waves:], total[waves:] + turned[:waves]], axis=0
    )
    for part, target in enumerate((own, one, two, three)):
        target[0] = bem
        target[1] = traces[:channels, part * 128 : (part + 1) * 128]


def front(upsample, counts, volume, density, matrix, cells, rows):
    channels = density.shape[0]
    message = pltpu.VMEM((2, channels, 128), F32)
    return pl.pallas_call(
        front_kernel,
        in_specs=[SMEM, SMEM] + [VMEM] * 3 + [HBM] * 2,
        out_specs=[VMEM] * 5,
        out_shape=[message] * 4 + [pltpu.VMEM((256, 512), BF16)],
        scratch_shapes=[
            pltpu.VMEM(density.shape, F32),
            pltpu.VMEM((UMAX, 2) + matrix.shape[2:], BF16),
            pltpu.SemaphoreType.DMA((UMAX + 1,)),
        ],
        compiler_params=LIMIT,
        name="front",
    )(upsample, counts, near(volume), near(cells), near(rows), afar(density), afar(matrix))


def edges_kernel(before, after, cross_in, corner, cross, sems):
    channels, size_x, _ = before.shape
    same_x, cross_x = sides_of(size_x)
    copies = []
    for k, face in enumerate((before, after)):
        copies.append(
            pltpu.make_async_copy(face.at[:, cross_x], cross.at[channels + k], sems.at[0, k])
        )
        copies.append(pltpu.make_async_copy(face.at[:, same_x], corner.at[k], sems.at[1, k]))
    run_all(copies)


def edges_of(before, after, cross):
    channels, _, size_z = before.shape
    return pl.pallas_call(
        edges_kernel,
        in_specs=[VMEM] * 3,
        out_specs=[VMEM] * 2,
        out_shape=[pltpu.VMEM((2, channels, size_z), F32), pltpu.VMEM(cross.shape, F32)],
        scratch_shapes=[pltpu.SemaphoreType.DMA((2, 2))],
        input_output_aliases={2: 1},
        compiler_params=LIMIT,
        name="edges",
    )(near(before), near(after), near(cross))


def join_kernel(own, one, two, three, out):
    group = 64
    lane = lax.broadcasted_iota(jnp.int32, own.shape[1:], 1)
    out[0] = jnp.where(lane < group, own[0], pltpu.roll(one[0], group, 1))
    out[1] = jnp.where(lane < group, two[0], pltpu.roll(three[0], group, 1))
    out[2] = (own[1] + one[1]) + (two[1] + three[1])


def join(own, one, two, three):
    return pl.pallas_call(
        join_kernel,
        in_specs=[VMEM] * 4,
        out_specs=VMEM,
        out_shape=pltpu.VMEM((3,) + own.shape[1:], F32),
        compiler_params=LIMIT,
        name="join",
    )(*[near(value) for value in (own, one, two, three)])


def y_sum(value, before, after):
    half = value.shape[0] // 2
    low, high = value[:half], value[half:]
    at = lax.broadcasted_iota(jnp.int32, low.shape, 0)
    low_down, high_down = pltpu.roll(low, 1, 0), pltpu.roll(high, 1, 0)
    low_up, high_up = pltpu.roll(low, half - 1, 0), pltpu.roll(high, half - 1, 0)
    first, final_row = at == 0, at == half - 1
    low_sum = jnp.where(first, before, low_down) + jnp.where(final_row, high_up, low_up)
    high_sum = jnp.where(first, low_down, high_down) + jnp.where(final_row, after, high_up)
    return jnp.concatenate([low_sum, high_sum], axis=0)


def z_sum(value):
    tiles = value.shape[1] // 128
    pieces = [value[:, 128 * k : 128 * (k + 1)] for k in range(tiles)]
    at = lax.broadcasted_iota(jnp.int32, pieces[0].shape, 1)
    first, final_lane = at == 0, at == 127
    down = [pltpu.roll(piece, 1, 1) for piece in pieces]
    up = [pltpu.roll(piece, 127, 1) for piece in pieces]
    sums = []
    for k in range(tiles):
        below = down[k - 1] if k > 0 else 0.0
        above = up[k + 1] if k < tiles - 1 else 0.0
        sums.append(jnp.where(first, below, down[k]) + jnp.where(final_lane, above, up[k]))
    return jnp.concatenate(sums, axis=1)


PLANES = 4


def interior_kernel(volume, given, before, after, *refs, first, prepares):
    if prepares:
        out, planes, tops, scales, buffers, sums, mixed, sems = refs
    else:
        _, out, planes, tops, buffers, sums, mixed, sems = refs
        scales = given
    parts, count, size_x, size_y, size_z = buffers.shape
    low = size_z - 128
    waves = volume.shape[1]

    if prepares:

        def prepare(x, carry):
            scale = given[0, x].astype(F32)
            scales[0, x] = scale * (8.0 / 3.0) - given[1, x].astype(F32)
            scales[1, x] = scale * (1.0 / 6.0)
            scales[2, x] = given[2, x].astype(F32)
            return carry

        lax.fori_loop(0, size_x, prepare, 0)
    nothing = jnp.zeros((size_y, size_z), F32)
    for part in range(parts):
        for x in (0, size_x + 1):
            sums[part, x] = nothing
            mixed[part, x] = nothing

    for step in range(count):
        wave = first + step

        def along(group, carry):
            for x in [group * PLANES + k for k in range(PLANES)]:
                for part in range(parts):
                    value = volume[part, wave, x]
                    channel = part * waves + wave
                    row = pl.ds(x, 1)
                    total = y_sum(value, before[channel, row, :], after[channel, row, :])
                    sums[part, x + 1] = total
                    mixed[part, x + 1] = 0.5 * total + value
            return carry

        def across(group, carry):
            for x in [group * PLANES + k for k in range(PLANES)]:
                own = []
                for part in range(parts):
                    level = (mixed[part, x] + mixed[part, x + 2]) + sums[part, x + 1]
                    own.append(z_sum(level) + (sums[part, x] + sums[part, x + 2]))
                real, imag = volume[0, wave, x], volume[1, wave, x]
                diagonal, sixth, absorb = scales[0, x], scales[1, x], scales[2, x]
                real_out = (diagonal * real - sixth * own[0]) + absorb * imag
                imag_out = (diagonal * imag - sixth * own[1]) - absorb * real
                for part, result in enumerate((real_out, imag_out)):
                    buffers[part, step, x] = result
                    tops[part, step, x] = result[:, low:]
            some = pl.ds(group * PLANES, PLANES)
            for part in range(parts):
                pltpu.make_async_copy(
                    buffers.at[part, step, some], out.at[part, wave, some], sems.at[part, step]
                ).start()
            return carry

        lax.fori_loop(0, size_x // PLANES, along, 0)
        lax.fori_loop(0, size_x // PLANES, across, 0)
        for part in range(parts):
            planes[0, part, step] = buffers[part, step, 0]
            planes[1, part, step] = buffers[part, step, size_x - 1]
    for step in range(count):
        for part in range(parts):
            pltpu.make_async_copy(
                buffers.at[part, step], out.at[part, first + step], sems.at[part, step]
            ).wait()


def interior(volume, given, before, after, first, count, previous=None):
    parts, _, size_x, size_y, size_z = volume.shape
    prepares = previous is None
    operands = [near(value) for value in (volume, given, before, after)]
    specs = [VMEM] * 4
    aliases = {}
    results = [
        jax.ShapeDtypeStruct(volume.shape, F32),
        pltpu.VMEM((2, parts, count, size_y, size_z), F32),
        pltpu.VMEM((parts, count, size_x, size_y, 128), F32),
    ]
    if prepares:
        results.append(pltpu.VMEM((3, size_x, size_y, size_z), F32))
    else:
        specs.append(ANY)
        operands.append(previous)
        aliases = {4: 0}
    work = pltpu.VMEM((parts, size_x + 2, size_y, size_z), F32)
    return pl.pallas_call(
        partial(interior_kernel, first=first, prepares=prepares),
        in_specs=specs,
        out_specs=[ANY] + [VMEM] * (len(results) - 1),
        out_shape=results,
        scratch_shapes=[
            pltpu.VMEM((parts, count, size_x, size_y, size_z), F32),
            work,
            work,
            pltpu.SemaphoreType.DMA((parts, count)),
        ],
        input_output_aliases=aliases,
        compiler_params=LIMIT,
        name="interior",
    )(*operands)


def side_kernel(scales, plane, ends, *refs, side):
    begun, out = refs[:CALLS], refs[CALLS]
    channels = out.shape[0]
    waves = channels // 2
    count = waves // CALLS
    size_x = scales.shape[1]
    place = sides_of(size_x)[side]
    end = jnp.where(place == 0, 0, 1)
    base = ends.shape[0] - 2
    scale = 0.5 * scales[1, place]
    for channel in range(channels):
        part, wave = divmod(channel, waves)
        value = plane[channel]
        low, high = [ends[base + k, pl.ds(channel, 1), :] for k in range(2)]
        total = y_sum(value, low, high)
        nearby = z_sum(total + (value + value)) + (total + total)
        out[channel] = begun[wave // count][end, part, wave % count] - scale * nearby


def one_side(scales, plane, ends, begun, side):
    size_y, size_z = scales.shape[2], scales.shape[3]
    return pl.pallas_call(
        partial(side_kernel, side=side),
        in_specs=[VMEM] * (3 + CALLS),
        out_specs=VMEM,
        out_shape=pltpu.VMEM((begun[0].shape[1] * begun[0].shape[2] * CALLS, size_y, size_z), F32),
        compiler_params=LIMIT,
        name="side",
    )(*[near(value) for value in (scales, plane, ends, *begun)])


def final_kernel(same, cross, zero, one, two, three, counted, *refs):
    begun = refs[:CALLS]
    out, boundary, planes, tops, sems = refs[CALLS + 1 :]
    narrow = lax.axis_index("narrow")
    channels, size_x, size_y, size_z = out.shape
    places = sides_of(size_x)
    last = size_x - 1
    low = size_z - 128
    waves = channels // 2
    count = waves // CALLS

    group = 64
    lane = lax.broadcasted_iota(jnp.int32, (channels, 128), 1)
    blocks = []
    for pair in range(2):
        close = zero[pair] + one[pair]
        distant = two[pair] + three[pair]
        blocks.append(jnp.where(lane < group, close, pltpu.roll(distant, group, 1)))
        blocks.append(jnp.where(lane < group, pltpu.roll(close, group, 1), distant))
    rows = three_rows(jnp.concatenate(blocks, axis=1))
    added = sum_of_three(
        lax.dot_general(rows, counted[...], NT, preferred_element_type=F32)
    )
    added = jnp.concatenate([added, jnp.zeros((128 - channels, added.shape[1]), F32)], axis=0).T
    at_top = lax.broadcasted_iota(jnp.int32, added.shape, 1) == 127

    copies = []
    even = places[1] == 0
    for channel in range(channels):
        part, wave = divmod(channel, waves)
        lifted = jnp.where(at_top, pltpu.roll(added, 127 - channel, 1), 0.0)
        lifted = lifted.reshape(size_x, size_y, 128)
        raised = (
            jnp.where(even, lifted[last], lifted[0]),
            jnp.where(even, lifted[0], lifted[last]),
        )
        for side, source in enumerate((same, cross)):
            planes[side, channel, :, pl.ds(0, low)] = source[channel, :, pl.ds(0, low)]
            planes[side, channel, :, pl.ds(low, 128)] = (
                source[channel, :, pl.ds(low, 128)] + raised[side]
            )
            copies.append(
                pltpu.make_async_copy(
                    planes.at[side, channel], out.at[channel, places[side]], sems.at[side, channel]
                )
            )
            copies[-1].start()
        tops[channel] = (
            begun[wave // count][part, wave % count, pl.ds(1, size_x - 2)] + lifted[1:last]
        )
        copies.append(
            pltpu.make_async_copy(
                tops.at[channel],
                out.at[channel, pl.ds(1, size_x - 2), :, pl.ds(low, 128)],
                sems.at[2, channel],
            )
        )
        copies[-1].start()

    trace = (zero[2] + one[2]) + pltpu.roll(two[2] + three[2], group, 1)
    mine = pltpu.roll(blocks[0] - 0.25 * trace, (128 - narrow * 4) % 128, 1).T
    boundary[0] = mine[:4, :waves]
    boundary[1] = mine[:4, waves:]
    for copy in copies:
        copy.wait()


def final(same, cross, messages, counted, begun, started):
    channels, size_x, size_y, size_z = started.shape
    close = [near(v) for v in (same, cross, *messages, counted, *begun)]
    return pl.pallas_call(
        final_kernel,
        in_specs=[VMEM] * len(close) + [ANY],
        out_specs=[ANY, VMEM],
        out_shape=[
            jax.ShapeDtypeStruct(started.shape, F32),
            jax.ShapeDtypeStruct((2, 4, channels // 2), F32),
        ],
        scratch_shapes=[
            pltpu.VMEM((2, channels, size_y, size_z), F32),
            pltpu.VMEM((channels, size_x - 2, size_y, 128), F32),
            pltpu.SemaphoreType.DMA((3, channels)),
        ],
        input_output_aliases={len(close): 0},
        compiler_params=LIMIT,
        name="final",
    )(*close, started)


N_WIDE = 8
N_NARROW = 16
AXES = ("wide", "narrow")


def moved(value, rule):
    pairs = []
    for wide in range(N_WIDE):
        for narrow in range(N_NARROW):
            target = rule(wide, narrow)
            if target is not None and 0 <= target[0] < N_WIDE and 0 <= target[1] < N_NARROW:
                pairs.append((wide * N_NARROW + narrow, target[0] * N_NARROW + target[1]))
    return lax.ppermute(value, AXES, pairs)


def along_y(step):
    return lambda w, n: (w ^ (step >> 1), n ^ ((step & 1) * 8))


def on_device(
    volume_field,
    coefficients,
    density,
    boundary_matrix,
    upsample,
    trace_cell,
    trace_row,
    slot_counts,
):
    parts, waves, size_x, size_y, size_z = volume_field.shape
    channels = parts * waves
    volume = volume_field.reshape(channels, size_x, size_y, size_z)

    upward, downward, same_out, cross_out = faces(volume)
    before = moved(upward, lambda w, n: (w, n + 1))
    after = moved(downward, lambda w, n: (w, n - 1))
    same_plane = moved(same_out, lambda w, n: (w ^ 1, n))

    own, one, two, three, counted = front(
        upsample,
        slot_counts,
        volume,
        density.reshape(channels, density.shape[2]),
        boundary_matrix,
        trace_cell.reshape(1, -1),
        trace_row.reshape(1, -1),
    )
    got = [
        moved(message, lambda w, n, s=step: (w ^ (2 * s), n))
        for step, message in ((1, one), (2, two), (3, three))
    ]
    corner_out, cross_out = edges_of(before, after, cross_out)
    corner = moved(corner_out, lambda w, n: (w ^ 1, n))
    cross_plane = moved(cross_out, lambda w, n: (w + (1 if w % 2 else -1), n))

    count = waves // CALLS
    started, planes, top, scales = interior(volume_field, coefficients, before, after, 0, count)
    planes, tops = [planes], [top]
    small = join(own, *got)
    for call, step in enumerate((2, 4, 1)):
        started, plane, top = interior(
            volume_field, scales, before, after, (call + 1) * count, count, started
        )
        planes.append(plane)
        tops.append(top)
        small = small + moved(small, lambda w, n, s=step: (w, n ^ s))
    messages = [small] + [moved(small, along_y(step)) for step in range(1, 4)]
    same = one_side(scales, same_plane, corner, planes, 0)
    cross = one_side(scales, cross_plane, cross_plane, planes, 1)

    volume_out, boundary = final(
        same, cross, messages, counted, tops, started.reshape(volume.shape)
    )
    return volume_out.reshape(volume_field.shape), boundary.transpose(0, 2, 1)


def solution(mesh):
    return jax.shard_map(
        on_device,
        mesh=mesh,
        in_specs=(
            P(None, None, "wide", "narrow", None),
            P(None, "wide", "narrow", None),
            P(None, None, "narrow"),
            P(None, None, "wide", "narrow"),
            P("narrow"),
            P("wide", "narrow", None),
            P("wide", "narrow", None),
            P("wide", "narrow"),
        ),
        out_specs=(P(None, None, "wide", "narrow", None), P(None, None, ("wide", "narrow"))),
        check_vma=False,
    )
```

```python
from functools import partial

import jax
import jax.numpy as jnp
from jax import lax
from jax.experimental import pallas as pl
from jax.experimental.pallas import tpu as pltpu
from jax.sharding import PartitionSpec as P


UMAX = 4
CALLS = 4
F32 = jnp.float32
BF16 = jnp.bfloat16
NT = (((1,), (1,)), ((), ()))
NN = (((1,), (0,)), ((), ()))


def split3(value):
    high = value.astype(BF16)
    rest = value - high.astype(F32)
    middle = rest.astype(BF16)
    low = (rest - middle.astype(F32)).astype(BF16)
    return high, middle, low


def three_rows(value):
    return jnp.concatenate(split3(value), axis=0)


def sum_of_three(value):
    size = value.shape[0] // 3
    return (value[2 * size :] + value[size : 2 * size]) + value[:size]


VMEM = pl.BlockSpec(memory_space=pltpu.VMEM)
ANY = pl.BlockSpec(memory_space=pl.ANY)
HBM = pl.BlockSpec(memory_space=pltpu.HBM)
LIMIT = pltpu.CompilerParams(vmem_limit_bytes=30 << 20)
SMEM = pl.BlockSpec(memory_space=pltpu.SMEM)


def near(value):
    return pltpu.with_memory_space_constraint(value, pltpu.VMEM)


def afar(value):
    return pltpu.with_memory_space_constraint(value, pltpu.HBM)


def scalar(value):
    return pltpu.with_memory_space_constraint(value, pltpu.SMEM)


def sides_of(size_x):
    even = lax.axis_index("wide") % 2 == 0
    return jnp.where(even, size_x - 1, 0), jnp.where(even, 0, size_x - 1)


def run_all(copies):
    for copy in copies:
        copy.start()
    for copy in copies:
        copy.wait()


def is_even():
    return lax.axis_index("narrow") % 2 == 0


def faces_kernel(volume, inner, outer, same, cross, sems):
    channels, size_x, size_y, _ = volume.shape
    same_x, cross_x = sides_of(size_x)

    def narrow_copies(even):
        ends = (size_y - 1, 0) if even else (0, size_y - 1)
        return [
            pltpu.make_async_copy(volume.at[:, :, end], target, sems.at[k])
            for k, (end, target) in enumerate(zip(ends, (inner, outer)))
        ]

    def begin(even):
        for copy in narrow_copies(even):
            copy.start()

    pl.when(is_even())(partial(begin, True))
    pl.when(jnp.logical_not(is_even()))(partial(begin, False))
    run_all(
        [
            pltpu.make_async_copy(volume.at[:, same_x], same, sems.at[2]),
            pltpu.make_async_copy(volume.at[:, cross_x], cross.at[pl.ds(0, channels)], sems.at[3]),
        ]
    )
    for copy in narrow_copies(True):
        copy.wait()


def faces(volume):
    channels, size_x, size_y, size_z = volume.shape
    return pl.pallas_call(
        faces_kernel,
        in_specs=[HBM],
        out_specs=[VMEM] * 4,
        out_shape=[
            pltpu.VMEM((channels, size_x, size_z), F32),
            pltpu.VMEM((channels, size_x, size_z), F32),
            pltpu.VMEM((channels, size_y, size_z), F32),
            pltpu.VMEM((channels + 2, size_y, size_z), F32),
        ],
        scratch_shapes=[pltpu.SemaphoreType.DMA((4,))],
        compiler_params=LIMIT,
        name="faces",
    )(afar(volume))


def front_kernel(
    upsample, counts, volume, cells, rows, density, matrix,
    own, one, two, three, count_out, top, sem,
):
    wide = lax.axis_index("wide")
    top_copy = pltpu.make_async_copy(
        volume.at[:, :, :, pl.ds(volume.shape[3] - 128, 128)], top, sem
    )
    top_copy.start()
    channels, _, _, _ = volume.shape
    slots = cells.shape[1]
    cell_count, row_count = count_out.shape
    live = lax.broadcasted_iota(jnp.int32, (1, slots), 1) < counts[0, 0]
    cell_of = jnp.where(live, cells[...], -1)
    cell_hit = lax.broadcasted_iota(jnp.int32, (cell_count, slots), 0) == cell_of
    row_of = (rows[...] ^ (wide * (row_count // 8))).astype(F32)
    row_of = jnp.broadcast_to(row_of, (8, slots)).T[:, :1]
    row_hit = lax.broadcasted_iota(jnp.int32, (slots, row_count), 1).astype(F32) == row_of
    cell_hit = jnp.where(cell_hit, 1.0, 0.0).astype(BF16)
    row_hit = jnp.where(row_hit, 1.0, 0.0).astype(BF16)
    counted = lax.dot_general(cell_hit, row_hit, NN, preferred_element_type=F32).astype(BF16)
    count_out[...] = counted

    blocks = upsample.shape[0]
    width = density.shape[1] // blocks
    group = matrix.shape[2]
    lane = lax.broadcasted_iota(jnp.int32, (channels, width), 1)
    total = jnp.zeros((channels, 2 * group), F32)
    pairs = []
    for block in range(blocks):
        here = density[:, pl.ds(block * width, width)]
        following = jnp.where(lane == width - 1, here, pltpu.roll(here, width - 1, 1))
        factor = upsample[block]
        inverse = jnp.where(
            factor == 1, 1.0, jnp.where(factor == 2, 0.5, jnp.where(factor == 3, 1.0 / 3.0, 0.25))
        )
        pairs.append((here, following, factor, inverse))
    for level in range(UMAX):
        pieces = []
        for here, following, factor, inverse in pairs:
            share = jnp.where(level < factor, inverse, 0.0)
            blend = level * inverse
            fine = ((1.0 - blend) * share) * here + (blend * share) * following
            pieces.append(fine.astype(BF16))
        both = matrix[:, level].reshape(2 * group, matrix.shape[3])
        total = total + lax.dot_general(
            jnp.concatenate(pieces, axis=1), both, NT, preferred_element_type=F32
        )

    top_copy.wait()
    at = lax.broadcasted_iota(jnp.int32, (cell_count, 128), 1)
    tops = jnp.zeros((cell_count, 128), F32)
    for channel in range(channels):
        value = top[channel].reshape(cell_count, 128)
        tops = jnp.where(at == channel, pltpu.roll(value, (channel + 1) % 128, 1), tops)
    traces = sum_of_three(
        lax.dot_general(
            three_rows(tops.T[:channels]), counted, NN, preferred_element_type=F32
        )
    )

    waves = channels // 2
    turned = pltpu.roll(total, group, 1)
    bem = jnp.concatenate(
        [total[:waves] - turned[waves:], total[waves:] + turned[:waves]], axis=0
    )
    for part, target in enumerate((own, one, two, three)):
        target[0] = bem
        target[1] = traces[:channels, part * 128 : (part + 1) * 128]


def front(upsample, counts, volume, density, matrix, cells, rows):
    channels = density.shape[0]
    message = pltpu.VMEM((2, channels, 128), F32)
    return pl.pallas_call(
        front_kernel,
        in_specs=[SMEM, SMEM, HBM] + [VMEM] * 4,
        out_specs=[VMEM] * 5,
        out_shape=[message] * 4 + [pltpu.VMEM((256, 512), BF16)],
        scratch_shapes=[pltpu.VMEM(volume.shape[:3] + (128,), F32), pltpu.SemaphoreType.DMA],
        compiler_params=LIMIT,
        name="front",
    )(
        scalar(upsample),
        scalar(counts),
        afar(volume),
        near(cells),
        near(rows),
        near(density),
        near(matrix),
    )


def edges_kernel(inner, outer, cross_in, corner, cross, sems):
    channels, size_x, _ = inner.shape
    same_x, cross_x = sides_of(size_x)
    high = jnp.where(is_even(), 1, 0)
    copies = []
    for k, (face, end) in enumerate(((inner, high), (outer, 1 - high))):
        copies.append(
            pltpu.make_async_copy(face.at[:, cross_x], cross.at[channels + end], sems.at[0, k])
        )
        copies.append(pltpu.make_async_copy(face.at[:, same_x], corner.at[end], sems.at[1, k]))
    run_all(copies)


def edges_of(inner, outer, cross):
    channels, _, size_z = inner.shape
    return pl.pallas_call(
        edges_kernel,
        in_specs=[VMEM] * 3,
        out_specs=[VMEM] * 2,
        out_shape=[pltpu.VMEM((2, channels, size_z), F32), pltpu.VMEM(cross.shape, F32)],
        scratch_shapes=[pltpu.SemaphoreType.DMA((2, 2))],
        input_output_aliases={2: 1},
        compiler_params=LIMIT,
        name="edges",
    )(near(inner), near(outer), near(cross))


def join_kernel(own, one, two, three, out):
    group = 64
    lane = lax.broadcasted_iota(jnp.int32, own.shape[1:], 1)
    out[0] = jnp.where(lane < group, own[0], pltpu.roll(one[0], group, 1))
    out[1] = jnp.where(lane < group, two[0], pltpu.roll(three[0], group, 1))
    out[2] = (own[1] + one[1]) + (two[1] + three[1])


def join(own, one, two, three):
    return pl.pallas_call(
        join_kernel,
        in_specs=[VMEM] * 4,
        out_specs=VMEM,
        out_shape=pltpu.VMEM((3,) + own.shape[1:], F32),
        compiler_params=LIMIT,
        name="join",
    )(*[near(value) for value in (own, one, two, three)])


def y_sum(value, before, after):
    half = value.shape[0] // 2
    low, high = value[:half], value[half:]
    at = lax.broadcasted_iota(jnp.int32, low.shape, 0)
    low_down, high_down = pltpu.roll(low, 1, 0), pltpu.roll(high, 1, 0)
    low_up, high_up = pltpu.roll(low, half - 1, 0), pltpu.roll(high, half - 1, 0)
    first, final_row = at == 0, at == half - 1
    low_sum = jnp.where(first, before, low_down) + jnp.where(final_row, high_up, low_up)
    high_sum = jnp.where(first, low_down, high_down) + jnp.where(final_row, after, high_up)
    return jnp.concatenate([low_sum, high_sum], axis=0)


def z_sum(value):
    tiles = value.shape[1] // 128
    pieces = [value[:, 128 * k : 128 * (k + 1)] for k in range(tiles)]
    at = lax.broadcasted_iota(jnp.int32, pieces[0].shape, 1)
    first, final_lane = at == 0, at == 127
    down = [pltpu.roll(piece, 1, 1) for piece in pieces]
    up = [pltpu.roll(piece, 127, 1) for piece in pieces]
    sums = []
    for k in range(tiles):
        below = down[k - 1] if k > 0 else 0.0
        above = up[k + 1] if k < tiles - 1 else 0.0
        sums.append(jnp.where(first, below, down[k]) + jnp.where(final_lane, above, up[k]))
    return jnp.concatenate(sums, axis=1)


PLANES = 4


def inside(ref, first, count):
    size_x, size_z = ref.shape[2], ref.shape[4]
    return ref.at[
        :, pl.ds(first, count), pl.ds(1, size_x - 2), :, pl.ds(0, size_z - 128)
    ]


def interior_kernel(volume, given, inner, outer, *refs, first):
    if first == 0:
        result, scales, sums, mixed = refs
    else:
        previous, _, result, out, sums, mixed, sem = refs
        scales = given
    parts, count, size_x, size_y, size_z = result.shape
    waves = volume.shape[1]
    even = is_even()

    if first == 0:

        def prepare(x, carry):
            scale = given[0, x].astype(F32)
            scales[0, x] = scale * (8.0 / 3.0) - given[1, x].astype(F32)
            scales[1, x] = scale * (1.0 / 6.0)
            scales[2, x] = given[2, x].astype(F32)
            return carry

        lax.fori_loop(0, size_x, prepare, 0)
    else:
        writing = pltpu.make_async_copy(
            inside(previous, 0, count), inside(out, first - count, count), sem
        )
        writing.start()
    nothing = jnp.zeros((size_y, size_z), F32)
    for part in range(parts):
        for x in (0, size_x + 1):
            sums[part, x] = nothing
            mixed[part, x] = nothing

    for step in range(count):
        wave = first + step

        def along(group, carry):
            for x in [group * PLANES + k for k in range(PLANES)]:
                for part in range(parts):
                    value = volume[part, wave, x]
                    channel = part * waves + wave
                    row = pl.ds(x, 1)
                    one, two = inner[channel, row, :], outer[channel, row, :]
                    before, after = jnp.where(even, two, one), jnp.where(even, one, two)
                    total = y_sum(value, before, after)
                    sums[part, x + 1] = total
                    mixed[part, x + 1] = 0.5 * total + value
            return carry

        def across(group, carry):
            for x in [group * PLANES + k for k in range(PLANES)]:
                own = []
                for part in range(parts):
                    level = (mixed[part, x] + mixed[part, x + 2]) + sums[part, x + 1]
                    own.append(z_sum(level) + (sums[part, x] + sums[part, x + 2]))
                real, imag = volume[0, wave, x], volume[1, wave, x]
                diagonal, sixth, absorb = scales[0, x], scales[1, x], scales[2, x]
                result[0, step, x] = (diagonal * real - sixth * own[0]) + absorb * imag
                result[1, step, x] = (diagonal * imag - sixth * own[1]) - absorb * real
            return carry

        lax.fori_loop(0, size_x // PLANES, along, 0)
        lax.fori_loop(0, size_x // PLANES, across, 0)
    if first > 0:
        writing.wait()


def interior(volume, given, inner, outer, first, count, previous=None, out=None):
    parts, _, size_x, size_y, size_z = volume.shape
    operands = [near(value) for value in (volume, given, inner, outer)]
    specs = [VMEM] * 4
    work = pltpu.VMEM((parts, size_x + 2, size_y, size_z), F32)
    results = [pltpu.VMEM((parts, count, size_x, size_y, size_z), F32)]
    result_specs = [VMEM]
    scratch = [work, work]
    aliases = {}
    if first == 0:
        results.append(pltpu.VMEM((3, size_x, size_y, size_z), F32))
        result_specs.append(VMEM)
    else:
        operands.append(near(previous))
        specs.append(VMEM)
        scratch.append(pltpu.SemaphoreType.DMA)
        results.append(jax.ShapeDtypeStruct(volume.shape, F32))
        result_specs.append(HBM)
        if out is not None:
            operands.append(out)
            specs.append(HBM)
            aliases = {5: 1}
    return pl.pallas_call(
        partial(interior_kernel if first == 0 or out is not None else first_write, first=first),
        in_specs=specs,
        out_specs=result_specs,
        out_shape=results,
        scratch_shapes=scratch,
        input_output_aliases=aliases,
        compiler_params=LIMIT,
        name="interior",
    )(*operands)


def first_write(volume, given, inner, outer, previous, *refs, first):
    interior_kernel(volume, given, inner, outer, previous, None, *refs, first=first)


def sides_kernel(scales, same_plane, corner, cross_plane, *refs):
    begun = refs[:CALLS]
    _, out, tiles, planes, sems, sem = refs[CALLS:]
    _, channels, _, size_z = (2,) + same_plane.shape
    waves = channels // 2
    count = waves // CALLS
    size_x = scales.shape[1]
    low = size_z - 128
    places = sides_of(size_x)
    writing = pltpu.make_async_copy(
        inside(begun[-1], 0, count), inside(out, waves - count, count), sem
    )
    writing.start()
    copies = []
    for side, (plane, ends) in enumerate(((same_plane, corner), (cross_plane, cross_plane))):
        place = places[side]
        base = ends.shape[0] - 2
        scale = 0.5 * scales[1, place]
        for channel in range(channels):
            part, wave = divmod(channel, waves)
            value = plane[channel]
            before, after = [ends[base + k, pl.ds(channel, 1), :] for k in range(2)]
            total = y_sum(value, before, after)
            nearby = z_sum(total + (value + value)) + (total + total)
            result = begun[wave // count][part, wave % count, place] - scale * nearby
            planes[side, channel] = result[:, :low]
            tiles[side, channel] = result[:, low:]
            copies.append(
                pltpu.make_async_copy(
                    planes.at[side, channel],
                    out.at[part, wave, place, :, pl.ds(0, low)],
                    sems.at[side, channel],
                )
            )
            copies[-1].start()
    for copy in copies + [writing]:
        copy.wait()


def both_sides(scales, same_plane, corner, cross_plane, begun, out):
    channels, size_y, size_z = same_plane.shape
    return pl.pallas_call(
        sides_kernel,
        in_specs=[VMEM] * (4 + CALLS) + [HBM],
        out_specs=[HBM, VMEM],
        out_shape=[
            jax.ShapeDtypeStruct(out.shape, F32),
            pltpu.VMEM((2, channels, size_y, 128), F32),
        ],
        scratch_shapes=[
            pltpu.VMEM((2, channels, size_y, size_z - 128), F32),
            pltpu.SemaphoreType.DMA((2, channels)),
            pltpu.SemaphoreType.DMA,
        ],
        input_output_aliases={4 + CALLS: 0},
        compiler_params=LIMIT,
        name="sides",
    )(*[near(v) for v in (scales, same_plane, corner, cross_plane, *begun)], out)


def final_kernel(tiles, zero, one, two, three, counted, *refs):
    begun = refs[:CALLS]
    out, boundary, tops, sems = refs[CALLS + 1 :]
    narrow = lax.axis_index("narrow")
    _, waves, size_x, size_y, size_z = out.shape
    channels = 2 * waves
    places = sides_of(size_x)
    last = size_x - 1
    low = size_z - 128
    count = waves // CALLS

    group = 64
    lane = lax.broadcasted_iota(jnp.int32, (channels, 128), 1)
    blocks = []
    for pair in range(2):
        close = zero[pair] + one[pair]
        distant = two[pair] + three[pair]
        blocks.append(jnp.where(lane < group, close, pltpu.roll(distant, group, 1)))
        blocks.append(jnp.where(lane < group, pltpu.roll(close, group, 1), distant))
    rows = three_rows(jnp.concatenate(blocks, axis=1))
    added = sum_of_three(
        lax.dot_general(rows, counted[...], NT, preferred_element_type=F32)
    )
    added = jnp.concatenate([added, jnp.zeros((128 - channels, added.shape[1]), F32)], axis=0).T
    at_top = lax.broadcasted_iota(jnp.int32, added.shape, 1) == 127

    copies = []
    same_low = places[0] == 0
    for channel in range(channels):
        part, wave = divmod(channel, waves)
        lifted = jnp.where(at_top, pltpu.roll(added, 127 - channel, 1), 0.0)
        lifted = lifted.reshape(size_x, size_y, 128)
        inner = begun[wave // count][part, wave % count, pl.ds(1, size_x - 2), :, pl.ds(low, 128)]
        tops[channel, pl.ds(1, size_x - 2)] = inner + lifted[1:last]
        same, cross = tiles[0, channel], tiles[1, channel]
        tops[channel, 0] = jnp.where(same_low, same, cross) + lifted[0]
        tops[channel, last] = jnp.where(same_low, cross, same) + lifted[last]
        copies.append(
            pltpu.make_async_copy(
                tops.at[channel], out.at[part, wave, :, :, pl.ds(low, 128)], sems.at[channel]
            )
        )
        copies[-1].start()

    trace = (zero[2] + one[2]) + pltpu.roll(two[2] + three[2], group, 1)
    mine = pltpu.roll(blocks[0] - 0.25 * trace, (128 - narrow * 4) % 128, 1).T
    boundary[0] = mine[:4, :waves]
    boundary[1] = mine[:4, waves:]
    for copy in copies:
        copy.wait()


def final(tiles, messages, counted, begun, out):
    _, waves, size_x, size_y, _ = out.shape
    close = [near(v) for v in (tiles, *messages, counted, *begun)]
    return pl.pallas_call(
        final_kernel,
        in_specs=[VMEM] * len(close) + [HBM],
        out_specs=[HBM, VMEM],
        out_shape=[
            jax.ShapeDtypeStruct(out.shape, F32),
            jax.ShapeDtypeStruct((2, 4, waves), F32),
        ],
        scratch_shapes=[
            pltpu.VMEM((2 * waves, size_x, size_y, 128), F32),
            pltpu.SemaphoreType.DMA((2 * waves,)),
        ],
        input_output_aliases={len(close): 0},
        compiler_params=LIMIT,
        name="final",
    )(*close, out)


N_WIDE = 8
N_NARROW = 16
AXES = ("wide", "narrow")


def moved(value, rule):
    pairs = []
    for wide in range(N_WIDE):
        for narrow in range(N_NARROW):
            target = rule(wide, narrow)
            if target is not None and 0 <= target[0] < N_WIDE and 0 <= target[1] < N_NARROW:
                pairs.append((wide * N_NARROW + narrow, target[0] * N_NARROW + target[1]))
    return lax.ppermute(value, AXES, pairs)


def along_y(step):
    return lambda w, n: (w ^ (step >> 1), n ^ ((step & 1) * 8))


def on_device(
    volume_field,
    coefficients,
    density,
    boundary_matrix,
    upsample,
    trace_cell,
    trace_row,
    slot_counts,
):
    parts, waves, size_x, size_y, size_z = volume_field.shape
    channels = parts * waves
    volume = volume_field.reshape(channels, size_x, size_y, size_z)

    inner_out, outer_out, same_out, cross_out = faces(volume)
    inner = moved(inner_out, lambda w, n: (w, n ^ 1))
    outer = moved(outer_out, lambda w, n: (w, n + (1 if n % 2 else -1)))
    same_plane = moved(same_out, lambda w, n: (w ^ 1, n))

    own, one, two, three, counted = front(
        upsample,
        slot_counts,
        volume,
        density.reshape(channels, density.shape[2]),
        boundary_matrix,
        trace_cell.reshape(1, -1),
        trace_row.reshape(1, -1),
    )
    got = [
        moved(message, lambda w, n, s=step: (w ^ (2 * s), n))
        for step, message in ((1, one), (2, two), (3, three))
    ]
    corner_out, cross_out = edges_of(inner, outer, cross_out)
    corner = moved(corner_out, lambda w, n: (w ^ 1, n))
    cross_plane = moved(cross_out, lambda w, n: (w + (1 if w % 2 else -1), n))

    count = waves // CALLS
    result, scales = interior(volume_field, coefficients, inner, outer, 0, count)
    results, out = [result], None
    small = join(own, *got)
    for call, step in enumerate((2, 4, 1), 1):
        result, out = interior(
            volume_field, scales, inner, outer, call * count, count, results[-1], out
        )
        results.append(result)
        small = small + moved(small, lambda w, n, s=step: (w, n ^ s))
    messages = [small] + [moved(small, along_y(step)) for step in range(1, 4)]
    out, tiles = both_sides(scales, same_plane, corner, cross_plane, results, out)

    volume_out, boundary = final(tiles, messages, counted, results, out)
    return volume_out, boundary.transpose(0, 2, 1)


def solution(mesh):
    return jax.shard_map(
        on_device,
        mesh=mesh,
        in_specs=(
            P(None, None, "wide", "narrow", None),
            P(None, "wide", "narrow", None),
            P(None, None, "narrow"),
            P(None, None, "wide", "narrow"),
            P("narrow"),
            P("wide", "narrow", None),
            P("wide", "narrow", None),
            P("wide", "narrow"),
        ),
        out_specs=(P(None, None, "wide", "narrow", None), P(None, None, ("wide", "narrow"))),
        check_vma=False,
    )
```

```python
from functools import partial

import jax
import jax.numpy as jnp
from jax import lax
from jax.experimental import pallas as pl
from jax.experimental.pallas import tpu as pltpu
from jax.sharding import PartitionSpec as P


UMAX = 4
F32 = jnp.float32
BF16 = jnp.bfloat16
NT = (((1,), (1,)), ((), ()))
NN = (((1,), (0,)), ((), ()))


def split3(value):
    high = value.astype(BF16)
    rest = value - high.astype(F32)
    middle = rest.astype(BF16)
    low = (rest - middle.astype(F32)).astype(BF16)
    return high, middle, low


def three_rows(value):
    return jnp.concatenate(split3(value), axis=0)


def sum_of_three(value):
    size = value.shape[0] // 3
    return (value[2 * size :] + value[size : 2 * size]) + value[:size]


VMEM = pl.BlockSpec(memory_space=pltpu.VMEM)
SMEM = pl.BlockSpec(memory_space=pltpu.SMEM)
HBM = pl.BlockSpec(memory_space=pltpu.HBM)
LIMIT = pltpu.CompilerParams(vmem_limit_bytes=12 << 20)


def near(value):
    return pltpu.with_memory_space_constraint(value, pltpu.VMEM)


def afar(value):
    return pltpu.with_memory_space_constraint(value, pltpu.HBM)


def sides_of(size_x):
    even = lax.axis_index("wide") % 2 == 0
    return jnp.where(even, size_x - 1, 0), jnp.where(even, 0, size_x - 1)


def run_all(copies):
    for copy in copies:
        copy.start()
    for copy in copies:
        copy.wait()


def is_even():
    return lax.axis_index("narrow") % 2 == 0


def faces_kernel(volume, inner, outer, same, cross, sems):
    channels, size_x, size_y, _ = volume.shape
    same_x, cross_x = sides_of(size_x)

    def narrow_copies(even):
        ends = (size_y - 1, 0) if even else (0, size_y - 1)
        return [
            pltpu.make_async_copy(volume.at[:, :, end], target, sems.at[k])
            for k, (end, target) in enumerate(zip(ends, (inner, outer)))
        ]

    def begin(even):
        for copy in narrow_copies(even):
            copy.start()

    pl.when(is_even())(partial(begin, True))
    pl.when(jnp.logical_not(is_even()))(partial(begin, False))
    run_all(
        [
            pltpu.make_async_copy(volume.at[:, same_x], same, sems.at[2]),
            pltpu.make_async_copy(volume.at[:, cross_x], cross.at[pl.ds(0, channels)], sems.at[3]),
        ]
    )
    for copy in narrow_copies(True):
        copy.wait()


def faces(volume):
    channels, size_x, size_y, size_z = volume.shape
    return pl.pallas_call(
        faces_kernel,
        in_specs=[HBM],
        out_specs=[VMEM] * 4,
        out_shape=[
            pltpu.VMEM((channels, size_x, size_z), F32),
            pltpu.VMEM((channels, size_x, size_z), F32),
            pltpu.VMEM((channels, size_y, size_z), F32),
            pltpu.VMEM((channels + 2, size_y, size_z), F32),
        ],
        scratch_shapes=[pltpu.SemaphoreType.DMA((4,))],
        compiler_params=LIMIT,
        name="faces",
    )(afar(volume))


def front_kernel(
    upsample, counts, volume, cells, rows, density, matrix,
    own, one, two, three, count_out, top, sem,
):
    wide = lax.axis_index("wide")
    top_copy = pltpu.make_async_copy(
        volume.at[:, :, :, pl.ds(volume.shape[3] - 128, 128)], top, sem
    )
    top_copy.start()
    channels, _, _, _ = volume.shape
    blocks = upsample.shape[1]
    width = density.shape[1] // blocks
    group = matrix.shape[2]
    lane = lax.broadcasted_iota(jnp.int32, (channels, width), 1)
    total = jnp.zeros((channels, 2 * group), F32)
    factors = upsample[...]
    inverses = jnp.where(
        factors == 1, 1.0, jnp.where(factors == 2, 0.5, jnp.where(factors == 3, 1.0 / 3.0, 0.25))
    )
    pairs = []
    for block in range(blocks):
        here = density[:, pl.ds(block * width, width)]
        pairs.append(
            (here, jnp.where(lane == width - 1, here, pltpu.roll(here, width - 1, 1)))
        )
    for level in range(UMAX):
        shares = jnp.where(level < factors, inverses, 0.0)
        blends = level * inverses
        nears, fars = (1.0 - blends) * shares, blends * shares
        pieces = []
        for block, (here, following) in enumerate(pairs):
            at = slice(block, block + 1)
            fine = nears[:, at] * here + fars[:, at] * following
            pieces.append(fine.astype(BF16))
        both = matrix[:, level].reshape(2 * group, matrix.shape[3])
        total = total + lax.dot_general(
            jnp.concatenate(pieces, axis=1), both, NT, preferred_element_type=F32
        )

    slots = cells.shape[1]
    cell_count, row_count = count_out.shape
    live = lax.broadcasted_iota(jnp.int32, (1, slots), 1) < counts[0, 0]
    cell_of = jnp.where(live, cells[...], -1)
    cell_hit = lax.broadcasted_iota(jnp.int32, (cell_count, slots), 0) == cell_of
    row_of = (rows[...] ^ (wide * (row_count // 8))).astype(F32)
    row_of = jnp.broadcast_to(row_of, (8, slots)).T[:, :1]
    row_hit = lax.broadcasted_iota(jnp.int32, (slots, row_count), 1).astype(F32) == row_of
    cell_hit = jnp.where(cell_hit, 1.0, 0.0).astype(BF16)
    row_hit = jnp.where(row_hit, 1.0, 0.0).astype(BF16)
    counted = lax.dot_general(cell_hit, row_hit, NN, preferred_element_type=F32).astype(BF16)
    count_out[...] = counted

    top_copy.wait()
    at = lax.broadcasted_iota(jnp.int32, (cell_count, 128), 1)
    tops = jnp.zeros((cell_count, 128), F32)
    for channel in range(channels):
        value = top[channel].reshape(cell_count, 128)
        tops = jnp.where(at == channel, pltpu.roll(value, (channel + 1) % 128, 1), tops)
    traces = sum_of_three(
        lax.dot_general(
            three_rows(tops.T[:channels]), counted, NN, preferred_element_type=F32
        )
    )

    waves = channels // 2
    turned = pltpu.roll(total, group, 1)
    bem = jnp.concatenate(
        [total[:waves] - turned[waves:], total[waves:] + turned[:waves]], axis=0
    )
    for part, target in enumerate((own, one, two, three)):
        target[0] = bem
        target[1] = traces[:channels, part * 128 : (part + 1) * 128]


def front(upsample, counts, volume, density, matrix, cells, rows):
    channels = density.shape[0]
    message = pltpu.VMEM((2, channels, 128), F32)
    return pl.pallas_call(
        front_kernel,
        in_specs=[VMEM, SMEM, HBM] + [VMEM] * 4,
        out_specs=[VMEM] * 5,
        out_shape=[message] * 4 + [pltpu.VMEM((256, 512), BF16)],
        scratch_shapes=[
            pltpu.VMEM(volume.shape[:3] + (128,), F32),
            pltpu.SemaphoreType.DMA,
        ],
        compiler_params=LIMIT,
        name="front",
    )(
        near(upsample),
        counts,
        afar(volume),
        near(cells),
        near(rows),
        near(density),
        near(matrix),
    )


def edges_kernel(inner, outer, cross_in, corner, cross, sems):
    channels, size_x, _ = inner.shape
    same_x, cross_x = sides_of(size_x)
    high = jnp.where(is_even(), 1, 0)
    copies = []
    for k, (face, end) in enumerate(((inner, high), (outer, 1 - high))):
        copies.append(
            pltpu.make_async_copy(face.at[:, cross_x], cross.at[channels + end], sems.at[0, k])
        )
        copies.append(pltpu.make_async_copy(face.at[:, same_x], corner.at[end], sems.at[1, k]))
    run_all(copies)


def edges_of(inner, outer, cross):
    channels, _, size_z = inner.shape
    return pl.pallas_call(
        edges_kernel,
        in_specs=[VMEM] * 3,
        out_specs=[VMEM] * 2,
        out_shape=[pltpu.VMEM((2, channels, size_z), F32), pltpu.VMEM(cross.shape, F32)],
        scratch_shapes=[pltpu.SemaphoreType.DMA((2, 2))],
        input_output_aliases={2: 1},
        compiler_params=LIMIT,
        name="edges",
    )(near(inner), near(outer), near(cross))


def join_kernel(own, one, two, three, out):
    group = 64
    lane = lax.broadcasted_iota(jnp.int32, own.shape[1:], 1)
    out[0] = jnp.where(lane < group, own[0], pltpu.roll(one[0], group, 1))
    out[1] = jnp.where(lane < group, two[0], pltpu.roll(three[0], group, 1))
    out[2] = (own[1] + one[1]) + (two[1] + three[1])


def join(own, one, two, three):
    return pl.pallas_call(
        join_kernel,
        in_specs=[VMEM] * 4,
        out_specs=VMEM,
        out_shape=pltpu.VMEM((3,) + own.shape[1:], F32),
        compiler_params=LIMIT,
        name="join",
    )(*[near(value) for value in (own, one, two, three)])


def y_sum(value, before, after):
    half = value.shape[0] // 2
    low, high = value[:half], value[half:]
    at = lax.broadcasted_iota(jnp.int32, low.shape, 0)
    low_down, high_down = pltpu.roll(low, 1, 0), pltpu.roll(high, 1, 0)
    low_up, high_up = pltpu.roll(low, half - 1, 0), pltpu.roll(high, half - 1, 0)
    first, final_row = at == 0, at == half - 1
    low_sum = jnp.where(first, before, low_down) + jnp.where(final_row, high_up, low_up)
    high_sum = jnp.where(first, low_down, high_down) + jnp.where(final_row, after, high_up)
    return jnp.concatenate([low_sum, high_sum], axis=0)


def z_sum(value):
    tiles = value.shape[1] // 128
    pieces = [value[:, 128 * k : 128 * (k + 1)] for k in range(tiles)]
    at = lax.broadcasted_iota(jnp.int32, pieces[0].shape, 1)
    first, final_lane = at == 0, at == 127
    down = [pltpu.roll(piece, 1, 1) for piece in pieces]
    up = [pltpu.roll(piece, 127, 1) for piece in pieces]
    sums = []
    for k in range(tiles):
        below = down[k - 1] if k > 0 else 0.0
        above = up[k + 1] if k < tiles - 1 else 0.0
        sums.append(jnp.where(first, below, down[k]) + jnp.where(final_lane, above, up[k]))
    return jnp.concatenate(sums, axis=1)


PLANES = 4


def inside(ref, wave):
    size_x, size_z = ref.shape[2], ref.shape[4]
    return ref.at[:, wave, pl.ds(1, size_x - 2), :, pl.ds(0, size_z - 128)]


def interior_kernel(
    volume, coefficients, inner, outer, result, scales, out, sums, mixed, sems
):
    parts, waves, size_x, size_y, size_z = result.shape
    even = is_even()

    def prepare(x, carry):
        scale = coefficients[0, x].astype(F32)
        scales[0, x] = scale * (8.0 / 3.0) - coefficients[1, x].astype(F32)
        scales[1, x] = scale * (1.0 / 6.0)
        scales[2, x] = coefficients[2, x].astype(F32)
        return carry

    lax.fori_loop(0, size_x, prepare, 0)
    nothing = jnp.zeros((size_y, size_z), F32)
    for part in range(parts):
        for x in (0, size_x + 1):
            sums[part, x] = nothing
            mixed[part, x] = nothing

    def one_wave(wave, done):
        def along(group, carry):
            for x in [group * PLANES + k for k in range(PLANES)]:
                for part in range(parts):
                    value = volume[part, wave, x]
                    channel = part * waves + wave
                    row = pl.ds(x, 1)
                    one, two = inner[channel, row, :], outer[channel, row, :]
                    before, after = jnp.where(even, two, one), jnp.where(even, one, two)
                    total = y_sum(value, before, after)
                    sums[part, x + 1] = total
                    mixed[part, x + 1] = 0.5 * total + value
            return carry

        def across(group, carry):
            for x in [group * PLANES + k for k in range(PLANES)]:
                own = []
                for part in range(parts):
                    level = (mixed[part, x] + mixed[part, x + 2]) + sums[part, x + 1]
                    own.append(z_sum(level) + (sums[part, x] + sums[part, x + 2]))
                real, imag = volume[0, wave, x], volume[1, wave, x]
                diagonal, sixth, absorb = scales[0, x], scales[1, x], scales[2, x]
                result[0, wave, x] = (diagonal * real - sixth * own[0]) + absorb * imag
                result[1, wave, x] = (diagonal * imag - sixth * own[1]) - absorb * real
            return carry

        lax.fori_loop(0, size_x // PLANES, along, 0)
        lax.fori_loop(0, size_x // PLANES, across, 0)

        @pl.when(wave < waves - 1)
        def _():
            pltpu.make_async_copy(inside(result, wave), inside(out, wave), sems.at[wave]).start()

        return done

    lax.fori_loop(0, waves, one_wave, 0)
    for wave in range(waves - 1):
        pltpu.make_async_copy(inside(result, wave), inside(out, wave), sems.at[wave]).wait()


def interior(volume, coefficients, inner, outer):
    parts, waves, size_x, size_y, size_z = volume.shape
    work = pltpu.VMEM((parts, size_x + 2, size_y, size_z), F32)
    return pl.pallas_call(
        interior_kernel,
        in_specs=[VMEM] * 4,
        out_specs=[VMEM, VMEM, HBM],
        out_shape=[
            pltpu.VMEM(volume.shape, F32),
            pltpu.VMEM((3, size_x, size_y, size_z), F32),
            jax.ShapeDtypeStruct(volume.shape, F32),
        ],
        scratch_shapes=[work, work, pltpu.SemaphoreType.DMA((waves,))],
        compiler_params=LIMIT,
        name="interior",
    )(*[near(value) for value in (volume, coefficients, inner, outer)])


def sides_kernel(
    scales, same_plane, corner, cross_plane, begun, _, out, tiles, planes, sems, sem
):
    channels, _, size_z = same_plane.shape
    waves = channels // 2
    size_x = scales.shape[1]
    low = size_z - 128
    places = sides_of(size_x)
    writing = pltpu.make_async_copy(inside(begun, waves - 1), inside(out, waves - 1), sem)
    writing.start()
    copies = []
    for side, (plane, ends) in enumerate(((same_plane, corner), (cross_plane, cross_plane))):
        place = places[side]
        base = ends.shape[0] - 2
        scale = 0.5 * scales[1, place]
        for channel in range(channels):
            part, wave = divmod(channel, waves)
            value = plane[channel]
            before, after = [ends[base + k, pl.ds(channel, 1), :] for k in range(2)]
            total = y_sum(value, before, after)
            nearby = z_sum(total + (value + value)) + (total + total)
            result = begun[part, wave, place] - scale * nearby
            planes[side, channel] = result[:, :low]
            tiles[side, channel] = result[:, low:]
            copies.append(
                pltpu.make_async_copy(
                    planes.at[side, channel],
                    out.at[part, wave, place, :, pl.ds(0, low)],
                    sems.at[side, channel],
                )
            )
            copies[-1].start()
    for copy in copies + [writing]:
        copy.wait()


def both_sides(scales, same_plane, corner, cross_plane, begun, out):
    channels, size_y, size_z = same_plane.shape
    return pl.pallas_call(
        sides_kernel,
        in_specs=[VMEM] * 5 + [HBM],
        out_specs=[HBM, VMEM],
        out_shape=[
            jax.ShapeDtypeStruct(out.shape, F32),
            pltpu.VMEM((2, channels, size_y, 128), F32),
        ],
        scratch_shapes=[
            pltpu.VMEM((2, channels, size_y, size_z - 128), F32),
            pltpu.SemaphoreType.DMA((2, channels)),
            pltpu.SemaphoreType.DMA,
        ],
        input_output_aliases={5: 0},
        compiler_params=LIMIT,
        name="sides",
    )(*[near(v) for v in (scales, same_plane, corner, cross_plane, begun)], out)


def final_kernel(
    tiles, zero, one, two, three, counted, begun, _, out, boundary, tops, sems
):
    narrow = lax.axis_index("narrow")
    _, waves, size_x, size_y, size_z = out.shape
    channels = 2 * waves
    places = sides_of(size_x)
    last = size_x - 1
    low = size_z - 128

    group = 64
    lane = lax.broadcasted_iota(jnp.int32, (channels, 128), 1)
    blocks = []
    for pair in range(2):
        close = zero[pair] + one[pair]
        distant = two[pair] + three[pair]
        blocks.append(jnp.where(lane < group, close, pltpu.roll(distant, group, 1)))
        blocks.append(jnp.where(lane < group, pltpu.roll(close, group, 1), distant))
    rows = three_rows(jnp.concatenate(blocks, axis=1))
    added = sum_of_three(
        lax.dot_general(rows, counted[...], NT, preferred_element_type=F32)
    )
    added = jnp.concatenate([added, jnp.zeros((128 - channels, added.shape[1]), F32)], axis=0).T
    at_top = lax.broadcasted_iota(jnp.int32, added.shape, 1) == 127

    copies = []
    same_low = places[0] == 0
    for channel in range(channels):
        part, wave = divmod(channel, waves)
        lifted = jnp.where(at_top, pltpu.roll(added, 127 - channel, 1), 0.0)
        lifted = lifted.reshape(size_x, size_y, 128)
        inner = begun[part, wave, pl.ds(1, size_x - 2), :, pl.ds(low, 128)]
        tops[channel, pl.ds(1, size_x - 2)] = inner + lifted[1:last]
        same, cross = tiles[0, channel], tiles[1, channel]
        tops[channel, 0] = jnp.where(same_low, same, cross) + lifted[0]
        tops[channel, last] = jnp.where(same_low, cross, same) + lifted[last]
        copies.append(
            pltpu.make_async_copy(
                tops.at[channel], out.at[part, wave, :, :, pl.ds(low, 128)], sems.at[channel]
            )
        )
        copies[-1].start()

    trace = (zero[2] + one[2]) + pltpu.roll(two[2] + three[2], group, 1)
    mine = pltpu.roll(blocks[0] - 0.25 * trace, (128 - narrow * 4) % 128, 1).T
    boundary[0] = mine[:4, :waves]
    boundary[1] = mine[:4, waves:]
    for copy in copies:
        copy.wait()


def final(tiles, messages, counted, begun, out):
    _, waves, size_x, size_y, _ = out.shape
    close = [near(v) for v in (tiles, *messages, counted, begun)]
    return pl.pallas_call(
        final_kernel,
        in_specs=[VMEM] * len(close) + [HBM],
        out_specs=[HBM, VMEM],
        out_shape=[
            jax.ShapeDtypeStruct(out.shape, F32),
            jax.ShapeDtypeStruct((2, 4, waves), F32),
        ],
        scratch_shapes=[
            pltpu.VMEM((2 * waves, size_x, size_y, 128), F32),
            pltpu.SemaphoreType.DMA((2 * waves,)),
        ],
        input_output_aliases={len(close): 0},
        compiler_params=LIMIT,
        name="final",
    )(*close, out)


N_WIDE = 8
N_NARROW = 16
AXES = ("wide", "narrow")


def moved(value, rule):
    pairs = []
    for wide in range(N_WIDE):
        for narrow in range(N_NARROW):
            target = rule(wide, narrow)
            if target is not None and 0 <= target[0] < N_WIDE and 0 <= target[1] < N_NARROW:
                pairs.append((wide * N_NARROW + narrow, target[0] * N_NARROW + target[1]))
    return lax.ppermute(value, AXES, pairs)


def along_y(step):
    return lambda w, n: (w ^ (step >> 1), n ^ ((step & 1) * 8))


def on_device(
    volume_field,
    coefficients,
    density,
    boundary_matrix,
    upsample,
    trace_cell,
    trace_row,
    slot_counts,
):
    parts, waves, size_x, size_y, size_z = volume_field.shape
    channels = parts * waves
    volume = volume_field.reshape(channels, size_x, size_y, size_z)

    inner_out, outer_out, same_out, cross_out = faces(volume)
    inner = moved(inner_out, lambda w, n: (w, n ^ 1))
    outer = moved(outer_out, lambda w, n: (w, n + (1 if n % 2 else -1)))
    same_plane = moved(same_out, lambda w, n: (w ^ 1, n))

    own, one, two, three, counted = front(
        upsample.reshape(1, -1),
        slot_counts,
        volume,
        density.reshape(channels, density.shape[2]),
        boundary_matrix,
        trace_cell.reshape(1, -1),
        trace_row.reshape(1, -1),
    )
    got = [
        moved(message, lambda w, n, s=step: (w ^ (2 * s), n))
        for step, message in ((1, one), (2, two), (3, three))
    ]
    small = join(own, *got)
    for step in (2, 4, 1):
        small = small + moved(small, lambda w, n, s=step: (w, n ^ s))
    corner_out, cross_out = edges_of(inner, outer, cross_out)
    corner = moved(corner_out, lambda w, n: (w ^ 1, n))
    cross_plane = moved(cross_out, lambda w, n: (w + (1 if w % 2 else -1), n))
    result, scales, out = interior(volume_field, coefficients, inner, outer)
    messages = [small] + [moved(small, along_y(step)) for step in range(1, 4)]
    out, tiles = both_sides(scales, same_plane, corner, cross_plane, result, out)

    volume_out, boundary = final(tiles, messages, counted, result, out)
    return volume_out, boundary.transpose(0, 2, 1)


def solution(mesh):
    return jax.shard_map(
        on_device,
        mesh=mesh,
        in_specs=(
            P(None, None, "wide", "narrow", None),
            P(None, "wide", "narrow", None),
            P(None, None, "narrow"),
            P(None, None, "wide", "narrow"),
            P("narrow"),
            P("wide", "narrow", None),
            P("wide", "narrow", None),
            P("wide", "narrow"),
        ),
        out_specs=(P(None, None, "wide", "narrow", None), P(None, None, ("wide", "narrow"))),
        check_vma=False,
    )
```

```python
from functools import partial

import jax
import jax.numpy as jnp
from jax import lax
from jax.experimental import pallas as pl
from jax.experimental.pallas import tpu as pltpu
from jax.sharding import PartitionSpec as P


UMAX = 4
CALLS = 4
F32 = jnp.float32
BF16 = jnp.bfloat16
NT = (((1,), (1,)), ((), ()))
NN = (((1,), (0,)), ((), ()))


def split3(value):
    high = value.astype(BF16)
    rest = value - high.astype(F32)
    middle = rest.astype(BF16)
    low = (rest - middle.astype(F32)).astype(BF16)
    return high, middle, low


def three_rows(value):
    return jnp.concatenate(split3(value), axis=0)


def sum_of_three(value):
    size = value.shape[0] // 3
    return (value[2 * size :] + value[size : 2 * size]) + value[:size]


VMEM = pl.BlockSpec(memory_space=pltpu.VMEM)
ANY = pl.BlockSpec(memory_space=pl.ANY)
HBM = pl.BlockSpec(memory_space=pltpu.HBM)
LIMIT = pltpu.CompilerParams(vmem_limit_bytes=12 << 20)
SMEM = pl.BlockSpec(memory_space=pltpu.SMEM)


def near(value):
    return pltpu.with_memory_space_constraint(value, pltpu.VMEM)


def afar(value):
    return pltpu.with_memory_space_constraint(value, pltpu.HBM)


def sides_of(size_x):
    even = lax.axis_index("wide") % 2 == 0
    return jnp.where(even, size_x - 1, 0), jnp.where(even, 0, size_x - 1)


def run_all(copies):
    for copy in copies:
        copy.start()
    for copy in copies:
        copy.wait()


def is_even():
    return lax.axis_index("narrow") % 2 == 0


def faces_kernel(volume, inner, outer, same, cross, sems):
    channels, size_x, size_y, _ = volume.shape
    same_x, cross_x = sides_of(size_x)

    def narrow_copies(even):
        ends = (size_y - 1, 0) if even else (0, size_y - 1)
        return [
            pltpu.make_async_copy(volume.at[:, :, end], target, sems.at[k])
            for k, (end, target) in enumerate(zip(ends, (inner, outer)))
        ]

    def begin(even):
        for copy in narrow_copies(even):
            copy.start()

    pl.when(is_even())(partial(begin, True))
    pl.when(jnp.logical_not(is_even()))(partial(begin, False))
    run_all(
        [
            pltpu.make_async_copy(volume.at[:, same_x], same, sems.at[2]),
            pltpu.make_async_copy(volume.at[:, cross_x], cross.at[pl.ds(0, channels)], sems.at[3]),
        ]
    )
    for copy in narrow_copies(True):
        copy.wait()


def faces(volume):
    channels, size_x, size_y, size_z = volume.shape
    return pl.pallas_call(
        faces_kernel,
        in_specs=[HBM],
        out_specs=[VMEM] * 4,
        out_shape=[
            pltpu.VMEM((channels, size_x, size_z), F32),
            pltpu.VMEM((channels, size_x, size_z), F32),
            pltpu.VMEM((channels, size_y, size_z), F32),
            pltpu.VMEM((channels + 2, size_y, size_z), F32),
        ],
        scratch_shapes=[pltpu.SemaphoreType.DMA((4,))],
        compiler_params=LIMIT,
        name="faces",
    )(afar(volume))


def front_kernel(
    upsample, counts, volume, cells, rows, density, matrix,
    own, one, two, three, count_out, top, sem,
):
    wide = lax.axis_index("wide")
    top_copy = pltpu.make_async_copy(
        volume.at[:, :, :, pl.ds(volume.shape[3] - 128, 128)], top, sem
    )
    top_copy.start()
    channels, _, _, _ = volume.shape
    blocks = upsample.shape[1]
    width = density.shape[1] // blocks
    group = matrix.shape[2]
    lane = lax.broadcasted_iota(jnp.int32, (channels, width), 1)
    total = jnp.zeros((channels, 2 * group), F32)
    factors = upsample[...]
    inverses = jnp.where(
        factors == 1, 1.0, jnp.where(factors == 2, 0.5, jnp.where(factors == 3, 1.0 / 3.0, 0.25))
    )
    pairs = []
    for block in range(blocks):
        here = density[:, pl.ds(block * width, width)]
        pairs.append(
            (here, jnp.where(lane == width - 1, here, pltpu.roll(here, width - 1, 1)))
        )
    for level in range(UMAX):
        shares = jnp.where(level < factors, inverses, 0.0)
        blends = level * inverses
        nears, fars = (1.0 - blends) * shares, blends * shares
        pieces = []
        for block, (here, following) in enumerate(pairs):
            at = slice(block, block + 1)
            fine = nears[:, at] * here + fars[:, at] * following
            pieces.append(fine.astype(BF16))
        both = matrix[:, level].reshape(2 * group, matrix.shape[3])
        total = total + lax.dot_general(
            jnp.concatenate(pieces, axis=1), both, NT, preferred_element_type=F32
        )

    slots = cells.shape[1]
    cell_count, row_count = count_out.shape
    live = lax.broadcasted_iota(jnp.int32, (1, slots), 1) < counts[0, 0]
    cell_of = jnp.where(live, cells[...], -1)
    cell_hit = lax.broadcasted_iota(jnp.int32, (cell_count, slots), 0) == cell_of
    row_of = (rows[...] ^ (wide * (row_count // 8))).astype(F32)
    row_of = jnp.broadcast_to(row_of, (8, slots)).T[:, :1]
    row_hit = lax.broadcasted_iota(jnp.int32, (slots, row_count), 1).astype(F32) == row_of
    cell_hit = jnp.where(cell_hit, 1.0, 0.0).astype(BF16)
    row_hit = jnp.where(row_hit, 1.0, 0.0).astype(BF16)
    counted = lax.dot_general(cell_hit, row_hit, NN, preferred_element_type=F32).astype(BF16)
    count_out[...] = counted

    top_copy.wait()
    at = lax.broadcasted_iota(jnp.int32, (cell_count, 128), 1)
    tops = jnp.zeros((cell_count, 128), F32)
    for channel in range(channels):
        value = top[channel].reshape(cell_count, 128)
        tops = jnp.where(at == channel, pltpu.roll(value, (channel + 1) % 128, 1), tops)
    traces = sum_of_three(
        lax.dot_general(
            three_rows(tops.T[:channels]), counted, NN, preferred_element_type=F32
        )
    )

    waves = channels // 2
    turned = pltpu.roll(total, group, 1)
    bem = jnp.concatenate(
        [total[:waves] - turned[waves:], total[waves:] + turned[:waves]], axis=0
    )
    for part, target in enumerate((own, one, two, three)):
        target[0] = bem
        target[1] = traces[:channels, part * 128 : (part + 1) * 128]


def front(upsample, counts, volume, density, matrix, cells, rows):
    channels = density.shape[0]
    message = pltpu.VMEM((2, channels, 128), F32)
    return pl.pallas_call(
        front_kernel,
        in_specs=[VMEM, SMEM, HBM] + [VMEM] * 4,
        out_specs=[VMEM] * 5,
        out_shape=[message] * 4 + [pltpu.VMEM((256, 512), BF16)],
        scratch_shapes=[
            pltpu.VMEM(volume.shape[:3] + (128,), F32),
            pltpu.SemaphoreType.DMA,
        ],
        compiler_params=LIMIT,
        name="front",
    )(
        near(upsample),
        counts,
        afar(volume),
        near(cells),
        near(rows),
        near(density),
        near(matrix),
    )


def edges_kernel(inner, outer, cross_in, corner, cross, sems):
    channels, size_x, _ = inner.shape
    same_x, cross_x = sides_of(size_x)
    high = jnp.where(is_even(), 1, 0)
    copies = []
    for k, (face, end) in enumerate(((inner, high), (outer, 1 - high))):
        copies.append(
            pltpu.make_async_copy(face.at[:, cross_x], cross.at[channels + end], sems.at[0, k])
        )
        copies.append(pltpu.make_async_copy(face.at[:, same_x], corner.at[end], sems.at[1, k]))
    run_all(copies)


def edges_of(inner, outer, cross):
    channels, _, size_z = inner.shape
    return pl.pallas_call(
        edges_kernel,
        in_specs=[VMEM] * 3,
        out_specs=[VMEM] * 2,
        out_shape=[pltpu.VMEM((2, channels, size_z), F32), pltpu.VMEM(cross.shape, F32)],
        scratch_shapes=[pltpu.SemaphoreType.DMA((2, 2))],
        input_output_aliases={2: 1},
        compiler_params=LIMIT,
        name="edges",
    )(near(inner), near(outer), near(cross))


def attach_kernel(small, corner, out):
    out[: small.shape[0]] = small[...]
    tiles = corner.shape[2] // 128
    for k in range(2):
        for tile in range(tiles):
            out[small.shape[0] + tiles * k + tile] = corner[k, :, 128 * tile : 128 * (tile + 1)]


def attach(small, corner):
    return pl.pallas_call(
        attach_kernel,
        in_specs=[VMEM] * 2,
        out_specs=VMEM,
        out_shape=pltpu.VMEM((small.shape[0] + 2 * corner.shape[2] // 128,) + small.shape[1:], F32),
        compiler_params=LIMIT,
        name="attach",
    )(near(small), near(corner))


def join_kernel(own, one, two, three, out):
    group = 64
    lane = lax.broadcasted_iota(jnp.int32, own.shape[1:], 1)
    out[0] = jnp.where(lane < group, own[0], pltpu.roll(one[0], group, 1))
    out[1] = jnp.where(lane < group, two[0], pltpu.roll(three[0], group, 1))
    out[2] = (own[1] + one[1]) + (two[1] + three[1])


def join(own, one, two, three):
    return pl.pallas_call(
        join_kernel,
        in_specs=[VMEM] * 4,
        out_specs=VMEM,
        out_shape=pltpu.VMEM((3,) + own.shape[1:], F32),
        compiler_params=LIMIT,
        name="join",
    )(*[near(value) for value in (own, one, two, three)])


def y_sum(value, before, after):
    half = value.shape[0] // 2
    low, high = value[:half], value[half:]
    at = lax.broadcasted_iota(jnp.int32, low.shape, 0)
    low_down, high_down = pltpu.roll(low, 1, 0), pltpu.roll(high, 1, 0)
    low_up, high_up = pltpu.roll(low, half - 1, 0), pltpu.roll(high, half - 1, 0)
    first, final_row = at == 0, at == half - 1
    low_sum = jnp.where(first, before, low_down) + jnp.where(final_row, high_up, low_up)
    high_sum = jnp.where(first, low_down, high_down) + jnp.where(final_row, after, high_up)
    return jnp.concatenate([low_sum, high_sum], axis=0)


def z_sum(value):
    tiles = value.shape[1] // 128
    pieces = [value[:, 128 * k : 128 * (k + 1)] for k in range(tiles)]
    at = lax.broadcasted_iota(jnp.int32, pieces[0].shape, 1)
    first, final_lane = at == 0, at == 127
    down = [pltpu.roll(piece, 1, 1) for piece in pieces]
    up = [pltpu.roll(piece, 127, 1) for piece in pieces]
    sums = []
    for k in range(tiles):
        below = down[k - 1] if k > 0 else 0.0
        above = up[k + 1] if k < tiles - 1 else 0.0
        sums.append(jnp.where(first, below, down[k]) + jnp.where(final_lane, above, up[k]))
    return jnp.concatenate(sums, axis=1)


PLANES = 16


def inside(ref, first, count):
    size_x, size_z = ref.shape[2], ref.shape[4]
    return ref.at[
        :, pl.ds(first, count), pl.ds(1, size_x - 2), :, pl.ds(0, size_z - 128)
    ]


def interior_kernel(volume, given, inner, outer, *refs, first):
    if first == 0:
        result, scales, sums, mixed = refs
    else:
        previous, _, result, out, sums, mixed, sem = refs
        scales = given
    parts, count, size_x, size_y, size_z = result.shape
    waves = volume.shape[1]
    even = is_even()

    if first == 0:

        def prepare(x, carry):
            scale = given[0, x].astype(F32)
            scales[0, x] = scale * (8.0 / 3.0) - given[1, x].astype(F32)
            scales[1, x] = scale * (1.0 / 6.0)
            scales[2, x] = given[2, x].astype(F32)
            return carry

        lax.fori_loop(0, size_x, prepare, 0)
    else:
        writing = pltpu.make_async_copy(
            inside(previous, 0, count), inside(out, first - count, count), sem
        )
        writing.start()
    nothing = jnp.zeros((size_y, size_z), F32)
    for part in range(parts):
        for x in (0, size_x + 1):
            sums[part, x] = nothing
            mixed[part, x] = nothing

    for step in range(count):
        wave = first + step

        def along(group, carry):
            for x in [group * PLANES + k for k in range(PLANES)]:
                for part in range(parts):
                    value = volume[part, wave, x]
                    channel = part * waves + wave
                    row = pl.ds(x, 1)
                    one, two = inner[channel, row, :], outer[channel, row, :]
                    before, after = jnp.where(even, two, one), jnp.where(even, one, two)
                    total = y_sum(value, before, after)
                    sums[part, x + 1] = total
                    mixed[part, x + 1] = 0.5 * total + value
            return carry

        def across(group, carry):
            for x in [group * PLANES + k for k in range(PLANES)]:
                own = []
                for part in range(parts):
                    level = (mixed[part, x] + mixed[part, x + 2]) + sums[part, x + 1]
                    own.append(z_sum(level) + (sums[part, x] + sums[part, x + 2]))
                real, imag = volume[0, wave, x], volume[1, wave, x]
                diagonal, sixth, absorb = scales[0, x], scales[1, x], scales[2, x]
                result[0, step, x] = (diagonal * real - sixth * own[0]) + absorb * imag
                result[1, step, x] = (diagonal * imag - sixth * own[1]) - absorb * real
            return carry

        lax.fori_loop(0, size_x // PLANES, along, 0)
        lax.fori_loop(0, size_x // PLANES, across, 0)
    if first > 0:
        writing.wait()


def interior(volume, given, inner, outer, first, count, previous=None, out=None):
    parts, _, size_x, size_y, size_z = volume.shape
    operands = [near(value) for value in (volume, given, inner, outer)]
    specs = [VMEM] * 4
    work = pltpu.VMEM((parts, size_x + 2, size_y, size_z), F32)
    results = [pltpu.VMEM((parts, count, size_x, size_y, size_z), F32)]
    result_specs = [VMEM]
    scratch = [work, work]
    aliases = {}
    if first == 0:
        results.append(pltpu.VMEM((3, size_x, size_y, size_z), F32))
        result_specs.append(VMEM)
    else:
        operands.append(near(previous))
        specs.append(VMEM)
        scratch.append(pltpu.SemaphoreType.DMA)
        results.append(jax.ShapeDtypeStruct(volume.shape, F32))
        result_specs.append(HBM)
        if out is not None:
            operands.append(out)
            specs.append(HBM)
            aliases = {5: 1}
    return pl.pallas_call(
        partial(interior_kernel if first == 0 or out is not None else first_write, first=first),
        in_specs=specs,
        out_specs=result_specs,
        out_shape=results,
        scratch_shapes=scratch,
        input_output_aliases=aliases,
        compiler_params=LIMIT,
        name="interior",
    )(*operands)


def first_write(volume, given, inner, outer, previous, *refs, first):
    interior_kernel(volume, given, inner, outer, previous, None, *refs, first=first)


def sides_kernel(scales, same_plane, cross_plane, *refs):
    begun = refs[:CALLS]
    _, out, tiles, ends_out, planes, sems, sem = refs[CALLS:]
    _, channels, size_y, size_z = (2,) + same_plane.shape
    waves = channels // 2
    count = waves // CALLS
    size_x = scales.shape[1]
    low = size_z - 128
    places = sides_of(size_x)
    writing = pltpu.make_async_copy(
        inside(begun[-1], 0, count), inside(out, waves - count, count), sem
    )
    writing.start()
    copies = []
    for side, plane in enumerate((same_plane, cross_plane)):
        place = places[side]
        scale = 0.5 * scales[1, place]
        for channel in range(channels):
            part, wave = divmod(channel, waves)
            value = plane[channel]
            if side == 0:
                before, after = 0.0, 0.0
            else:
                before, after = [plane[channels + k, pl.ds(channel, 1), :] for k in range(2)]
            total = y_sum(value, before, after)
            nearby = z_sum(total + (value + value)) + (total + total)
            result = begun[wave // count][part, wave % count, place] - scale * nearby
            if side == 0:
                ends_out[0, part, pl.ds(wave, 1), :] = result[:1]
                ends_out[1, part, pl.ds(wave, 1), :] = result[size_y - 1 :]
            planes[side, channel] = result[:, :low]
            tiles[side, channel] = result[:, low:]
            copies.append(
                pltpu.make_async_copy(
                    planes.at[side, channel],
                    out.at[part, wave, place, :, pl.ds(0, low)],
                    sems.at[side, channel],
                )
            )
            copies[-1].start()
    for copy in copies + [writing]:
        copy.wait()


def both_sides(scales, same_plane, cross_plane, begun, out):
    channels, size_y, size_z = same_plane.shape
    return pl.pallas_call(
        sides_kernel,
        in_specs=[VMEM] * (3 + CALLS) + [HBM],
        out_specs=[HBM, VMEM, VMEM],
        out_shape=[
            jax.ShapeDtypeStruct(out.shape, F32),
            pltpu.VMEM((2, channels, size_y, 128), F32),
            pltpu.VMEM((2, 2, channels // 2, size_z), F32),
        ],
        scratch_shapes=[
            pltpu.VMEM((2, channels, size_y, size_z - 128), F32),
            pltpu.SemaphoreType.DMA((2, channels)),
            pltpu.SemaphoreType.DMA,
        ],
        input_output_aliases={3 + CALLS: 0},
        compiler_params=LIMIT,
        name="sides",
    )(*[near(v) for v in (scales, same_plane, cross_plane, *begun)], out)


def final_kernel(scales, tiles, ends, zero, one, two, three, counted, *refs):
    begun = refs[:CALLS]
    out, boundary, tops, edge_rows, sems, edge_sems = refs[CALLS + 1 :]
    narrow = lax.axis_index("narrow")
    _, waves, size_x, size_y, size_z = out.shape
    channels = 2 * waves
    places = sides_of(size_x)
    last = size_x - 1
    low = size_z - 128
    count = waves // CALLS

    group = 64
    lane = lax.broadcasted_iota(jnp.int32, (channels, 128), 1)
    blocks = []
    for pair in range(2):
        close = zero[pair] + one[pair]
        distant = two[pair] + three[pair]
        blocks.append(jnp.where(lane < group, close, pltpu.roll(distant, group, 1)))
        blocks.append(jnp.where(lane < group, pltpu.roll(close, group, 1), distant))
    rows = three_rows(jnp.concatenate(blocks, axis=1))
    added = sum_of_three(
        lax.dot_general(rows, counted[...], NT, preferred_element_type=F32)
    )
    added = jnp.concatenate([added, jnp.zeros((128 - channels, added.shape[1]), F32)], axis=0).T
    at_top = lax.broadcasted_iota(jnp.int32, added.shape, 1) == 127

    copies = []
    same_low = places[0] == 0
    bits = []
    for k, end in enumerate((0, size_y - 1)):
        value = jnp.concatenate(
            [two[3 + (size_z // 128) * k + tile] for tile in range(size_z // 128)], axis=1
        )
        scale = 0.5 * scales[1, places[0], pl.ds(end, 1), :]
        extra = scale * (z_sum(value) + (value + value))
        bits.append(extra[:, low:])
        for part in range(2):
            edge_rows[k, part] = (ends[k, part] - extra[part * waves : (part + 1) * waves])[:, :low]
        copies.append(
            pltpu.make_async_copy(
                edge_rows.at[k], out.at[:, :, places[0], end, pl.ds(0, low)], edge_sems.at[k]
            )
        )
        copies[-1].start()
    row = lax.broadcasted_iota(jnp.int32, (size_y, 128), 0)
    for channel in range(channels):
        part, wave = divmod(channel, waves)
        lifted = jnp.where(at_top, pltpu.roll(added, 127 - channel, 1), 0.0)
        lifted = lifted.reshape(size_x, size_y, 128)
        inner = begun[wave // count][part, wave % count, pl.ds(1, size_x - 2), :, pl.ds(low, 128)]
        tops[channel, pl.ds(1, size_x - 2)] = inner + lifted[1:last]
        same, cross = tiles[0, channel], tiles[1, channel]
        first, final_row = bits[0][channel : channel + 1], bits[1][channel : channel + 1]
        same = same - jnp.where(row == 0, first, jnp.where(row == size_y - 1, final_row, 0.0))
        tops[channel, 0] = jnp.where(same_low, same, cross) + lifted[0]
        tops[channel, last] = jnp.where(same_low, cross, same) + lifted[last]
        copies.append(
            pltpu.make_async_copy(
                tops.at[channel], out.at[part, wave, :, :, pl.ds(low, 128)], sems.at[channel]
            )
        )
        copies[-1].start()

    trace = (zero[2] + one[2]) + pltpu.roll(two[2] + three[2], group, 1)
    mine = pltpu.roll(blocks[0] - 0.25 * trace, (128 - narrow * 4) % 128, 1).T
    boundary[0] = mine[:4, :waves]
    boundary[1] = mine[:4, waves:]
    for copy in copies:
        copy.wait()


def final(scales, tiles, ends, messages, counted, begun, out):
    _, waves, size_x, size_y, size_z = out.shape
    close = [near(v) for v in (scales, tiles, ends, *messages, counted, *begun)]
    return pl.pallas_call(
        final_kernel,
        in_specs=[VMEM] * len(close) + [HBM],
        out_specs=[HBM, VMEM],
        out_shape=[
            jax.ShapeDtypeStruct(out.shape, F32),
            jax.ShapeDtypeStruct((2, 4, waves), F32),
        ],
        scratch_shapes=[
            pltpu.VMEM((2 * waves, size_x, size_y, 128), F32),
            pltpu.VMEM((2, 2, waves, size_z - 128), F32),
            pltpu.SemaphoreType.DMA((2 * waves,)),
            pltpu.SemaphoreType.DMA((2,)),
        ],
        input_output_aliases={len(close): 0},
        compiler_params=LIMIT,
        name="final",
    )(*close, out)


N_WIDE = 8
N_NARROW = 16
AXES = ("wide", "narrow")


def moved(value, rule):
    pairs = []
    for wide in range(N_WIDE):
        for narrow in range(N_NARROW):
            target = rule(wide, narrow)
            if target is not None and 0 <= target[0] < N_WIDE and 0 <= target[1] < N_NARROW:
                pairs.append((wide * N_NARROW + narrow, target[0] * N_NARROW + target[1]))
    return lax.ppermute(value, AXES, pairs)


def along_y(step):
    return lambda w, n: (w ^ (step >> 1), n ^ ((step & 1) * 8))


def on_device(
    volume_field,
    coefficients,
    density,
    boundary_matrix,
    upsample,
    trace_cell,
    trace_row,
    slot_counts,
):
    parts, waves, size_x, size_y, size_z = volume_field.shape
    channels = parts * waves
    volume = volume_field.reshape(channels, size_x, size_y, size_z)

    inner_out, outer_out, same_out, cross_out = faces(volume)
    inner = moved(inner_out, lambda w, n: (w, n ^ 1))
    outer = moved(outer_out, lambda w, n: (w, n + (1 if n % 2 else -1)))
    same_plane = moved(same_out, lambda w, n: (w ^ 1, n))

    own, one, two, three, counted = front(
        upsample.reshape(1, -1),
        slot_counts,
        volume,
        density.reshape(channels, density.shape[2]),
        boundary_matrix,
        trace_cell.reshape(1, -1),
        trace_row.reshape(1, -1),
    )
    got = [
        moved(message, lambda w, n, s=step: (w ^ (2 * s), n))
        for step, message in ((1, one), (2, two), (3, three))
    ]
    corner_out, cross_out = edges_of(inner, outer, cross_out)
    cross_plane = moved(cross_out, lambda w, n: (w + (1 if w % 2 else -1), n))

    count = waves // CALLS
    result, scales = interior(volume_field, coefficients, inner, outer, 0, count)
    results, out = [result], None
    small = join(own, *got)
    for call, step in enumerate((2, 4, 1), 1):
        result, out = interior(
            volume_field, scales, inner, outer, call * count, count, results[-1], out
        )
        results.append(result)
        small = small + moved(small, lambda w, n, s=step: (w, n ^ s))
    with_corner = attach(small, corner_out)
    messages = [small] + [
        moved(message, along_y(step))
        for step, message in ((1, small), (2, with_corner), (3, small))
    ]
    out, tiles, ends = both_sides(scales, same_plane, cross_plane, results, out)

    volume_out, boundary = final(scales, tiles, ends, messages, counted, results, out)
    return volume_out, boundary.transpose(0, 2, 1)


def solution(mesh):
    return jax.shard_map(
        on_device,
        mesh=mesh,
        in_specs=(
            P(None, None, "wide", "narrow", None),
            P(None, "wide", "narrow", None),
            P(None, None, "narrow"),
            P(None, None, "wide", "narrow"),
            P("narrow"),
            P("wide", "narrow", None),
            P("wide", "narrow", None),
            P("wide", "narrow"),
        ),
        out_specs=(P(None, None, "wide", "narrow", None), P(None, None, ("wide", "narrow"))),
        check_vma=False,
    )
```
